256 devices in a mesh: dp: 32 (over z_lo, x, core), mp: 8 (over z_hi, y).
Axes of the slice: x: 4, y: 4, z: 8 (z_hi: 2, z_lo: 4; z = z_hi * 4 + z_lo), core: 2. Of those that a mesh axis runs over, the one named last changes fastest.
Arguments:
- clean: bfloat16 [32, 1024, 1280], P('dp', 'mp'), may hold values from -6 to 6
- noise: bfloat16 [32, 1024, 1280], P('dp', 'mp'), may hold values from -6 to 6
- tsteps: int32 [32], P('dp'), may hold values from 0 to 999
- alpha_tab: float32 [1000], replicated, may hold values from 0.3 to 0.99
- weight_tab: float32 [1000], replicated, may hold values from 0.1 to 3
- norm1_gain: float32 [1280], replicated, may hold values from 0.1 to 1.9
- norm2_gain: float32 [1280], replicated, may hold values from 0.1 to 1.9
- wqkv: bfloat16 [3, 1280, 1280], P(None, 'dp', 'mp'), may hold values from -4 to 4
- wout: bfloat16 [1280, 1280], P('dp', 'mp'), may hold values from -0.625 to 0.625
- wgate: bfloat16 [1280, 5120], P('dp', 'mp'), may hold values from -0.15625 to 0.15625
- wvalue: bfloat16 [1280, 5120], P('dp', 'mp'), may hold values from -0.15625 to 0.15625
- wdown: bfloat16 [5120, 1280], P('mp', 'dp'), may hold values from -0.078125 to 0.078125
Outputs:
- denoised: float32 [32, 1024, 1280], P('dp', 'mp')
- loss: float32 [], replicated
The draws below stay inside these ranges and needn't reach their ends.
All inputs are finite; a program needn't handle non-finite values.
Results may differ from the reference program's by a relative error of at most 0.02.
Values may be sent and summed in bfloat16 or wider, within the bound.
A program may use at most 64 MiB of HBM per device.

```python
import math
import jax
import jax.numpy as jnp
from jax import lax

D = 1280
HEADS = 20
HEAD = 64
FF = 5120
L = 1024
TSTEPS = 1000
B = 32
N_MP = 8


def draw_wqkv(key, part):
    base_key = jax.random.fold_in(key, 11)
    weights = jnp.clip(jax.random.normal(base_key, (3, D, D), jnp.float32), -4.0, 4.0) * D ** (-0.5)
    return weights.astype(jnp.bfloat16)


def plant(values, stream_key, least, top_value):
    index_at = [jax.random.randint(jax.random.fold_in(stream_key, axis), (), 0, length) for axis, length in enumerate(values.shape)]
    widest = values.shape.index(max(values.shape))
    neighbour = index_at[:widest] + [(index_at[widest] + 1) % values.shape[widest]] + index_at[widest + 1:]
    return values.at[tuple(index_at)].set(least).at[tuple(neighbour)].set(top_value)


def block_levels(key, extent, shards, least, high):
    level = 1.0
    for position, blocks in shards:
        steps = jax.random.uniform(jax.random.fold_in(jax.random.fold_in(key, 6), position), (blocks,), jnp.float32, least / len(shards), high / len(shards))
        level = level * jnp.repeat(jnp.exp(steps), extent[position] // blocks).reshape((-1,) + (1,) * (len(extent) - 1 - position))
    return level


def gaussian(key, shape, deviation, limit, cuts=(), kind=jnp.bfloat16):
    array = deviation * jax.random.normal(key, shape, jnp.float32)
    if cuts:
        array = array * block_levels(key, shape, cuts, -0.22, 0.18)
    return jnp.clip(array, -limit, limit).astype(kind)


def setup_inputs(seed: int = 0) -> dict:
    streams_of = jax.random.split(jax.random.key(seed), 13)
    clean = gaussian(streams_of[0], (B, L, D), 1.0, 6.0, ((0, 32), (1, 8)))
    noise = gaussian(streams_of[1], (B, L, D), 1.0, 6.0, ((0, 32), (1, 8)))
    tsteps = plant(jax.random.randint(streams_of[2], (B,), 0, TSTEPS), jax.random.fold_in(streams_of[2], 1), 0, TSTEPS - 1).astype(jnp.int32)
    alpha_tab = jnp.clip(jnp.exp(jax.random.uniform(streams_of[3], (TSTEPS,), jnp.float32, math.log(0.3), math.log(0.99))), 0.3, 0.99)
    weight_tab = jnp.clip(jnp.exp(jax.random.uniform(streams_of[4], (TSTEPS,), jnp.float32, math.log(0.1), math.log(3.0))), 0.1, 3.0)
    norm1_gain = jnp.clip(1.0 + 0.18 * jax.random.normal(streams_of[5], (D,), jnp.float32), 0.1, 1.9)
    norm2_gain = jnp.clip(1.0 + 0.18 * jax.random.normal(streams_of[6], (D,), jnp.float32), 0.1, 1.9)
    wqkv = draw_wqkv(jax.random.fold_in(streams_of[12], 71), 0)
    wout = gaussian(streams_of[8], (D, D), (D // 16) ** -0.5, 0.625, ((0, 32), (1, 8)))
    wgate = gaussian(streams_of[9], (D, FF), D ** -0.5, 0.15625, ((0, 32), (1, 8)))
    wvalue = gaussian(streams_of[10], (D, FF), D ** -0.5, 0.15625, ((0, 32), (1, 8)))
    wdown = gaussian(streams_of[11], (FF, D), FF ** -0.5, 0.078125, ((0, 8), (1, 32)))
    return dict(clean=clean, noise=noise, tsteps=tsteps, alpha_tab=alpha_tab, weight_tab=weight_tab, norm1_gain=norm1_gain, norm2_gain=norm2_gain, wqkv=wqkv, wout=wout, wgate=wgate, wvalue=wvalue, wdown=wdown)


def lookup(steps, table):
    match = steps[:, None] == jnp.arange(table.shape[0], dtype=jnp.int32)[None, :]
    return lax.optimization_barrier(jnp.sum(jnp.where(match, table[None, :], jnp.zeros((), table.dtype)), axis=1))

def layer_norm(values, gain):
    wide = values.astype(jnp.float32)
    center = wide - lax.optimization_barrier(jnp.mean(wide, axis=-1, keepdims=True))
    spread = lax.optimization_barrier(jnp.mean(center * center, axis=-1, keepdims=True))
    return (center * lax.rsqrt(spread + 1e-05) * gain).astype(jnp.bfloat16)

def one_sample(noised_one, norm1_gain, norm2_gain, wqkv, wout, wgate, wvalue, wdown):
    normed1 = layer_norm(noised_one, norm1_gain)
    query = jnp.dot(normed1, wqkv[0], preferred_element_type=jnp.float32).astype(jnp.bfloat16)
    keys = jnp.dot(normed1, wqkv[1], preferred_element_type=jnp.float32).astype(jnp.bfloat16)
    values = jnp.dot(normed1, wqkv[2], preferred_element_type=jnp.float32).astype(jnp.bfloat16)
    q_heads = query.reshape(L, HEADS, HEAD).astype(jnp.float32)
    k_heads = keys.reshape(L, HEADS, HEAD).astype(jnp.float32)
    v_heads = values.reshape(L, HEADS, HEAD).astype(jnp.float32)
    scores = jnp.einsum('qhd,khd->hqk', q_heads, k_heads) * HEAD ** (-0.5)
    probs = jax.nn.softmax(scores, axis=-1).astype(jnp.bfloat16)
    mixed = jnp.einsum('hqk,khd->qhd', probs.astype(jnp.float32), v_heads).astype(jnp.bfloat16).reshape(L, D)
    resid = (noised_one.astype(jnp.float32) + jnp.dot(mixed, wout, preferred_element_type=jnp.float32)).astype(jnp.bfloat16)
    normed2 = layer_norm(resid, norm2_gain)
    gate = jnp.dot(normed2, wgate, preferred_element_type=jnp.float32)
    value = jnp.dot(normed2, wvalue, preferred_element_type=jnp.float32)
    hidden = (jax.nn.gelu(gate, approximate=False) * value).astype(jnp.bfloat16)
    blocks = jnp.einsum('lkf,kfd->kld', hidden.reshape(L, N_MP, FF // N_MP).astype(jnp.float32), wdown.reshape(N_MP, FF // N_MP, D).astype(jnp.float32))
    ff_out = lax.optimization_barrier(jnp.sum(blocks.astype(jnp.bfloat16).astype(jnp.float32), axis=0))
    return resid.astype(jnp.float32) + ff_out

def reference(clean, noise, tsteps, alpha_tab, weight_tab, norm1_gain, norm2_gain, wqkv, wout, wgate, wvalue, wdown):
    alpha = lookup(tsteps, alpha_tab)
    sigma = jnp.sqrt(1.0 - alpha * alpha)
    weight = lookup(tsteps, weight_tab)
    noised = (alpha[:, None, None] * clean.astype(jnp.float32) + sigma[:, None, None] * noise.astype(jnp.float32)).astype(jnp.bfloat16)

    def step_one(noised_one):
        return one_sample(noised_one, norm1_gain, norm2_gain, wqkv, wout, wgate, wvalue, wdown)
    prediction = lax.map(step_one, noised)
    denoised = (noised.astype(jnp.float32) - sigma[:, None, None] * prediction) / alpha[:, None, None]
    error = denoised - clean.astype(jnp.float32)
    per_sample = lax.optimization_barrier(jnp.mean(error * error, axis=(1, 2)))
    return (denoised, jnp.sum(weight * per_sample))
```

```python
import jax
import jax.numpy as jnp
from jax import lax
from jax.experimental import pallas as pl
from jax.experimental.pallas import tpu as pltpu
from jax.sharding import Mesh
from jax.sharding import PartitionSpec as P

D = 1280
HEAD = 64
L = 1024
ROWS = 128
AXES = ("zl", "x", "c", "zh", "y")
DP = ("zl", "x", "c")
MP = ("zh", "y")
MESH = pl.DeviceIdType.MESH
BF = jnp.bfloat16
F32 = jnp.float32
NT = (((1,), (1,)), ((), ()))


def lookup(steps, table):
    match = steps[:, None] == jnp.arange(table.shape[0], dtype=jnp.int32)[None, :]
    return jnp.sum(jnp.where(match, table[None, :], jnp.zeros((), table.dtype)), axis=1)


def normed(values, gain):
    wide = values.astype(F32)
    center = wide - jnp.mean(wide, axis=-1, keepdims=True)
    spread = jnp.mean(center * center, axis=-1, keepdims=True)
    return (center * lax.rsqrt(spread + 1e-05) * gain).astype(BF)


def kernel(
    clean, noise, scal, gains, keep, give,
    den, loss,
    recv, qs, wt, qw, w1, w2, n1, qkv, mo, mx, n2, hid, fs, ffin, noised, resid, l1, l2, l3,
    ss, rs, ls,
):
    zl, x, c, zh, y = (lax.axis_index(a) for a in AXES)
    z = zh * 4 + zl
    sends = []
    count = [0]

    def other(name, k, n):
        return {name: lax.rem(lax.axis_index(name) + k, n)}

    def zto(k):
        t = lax.rem(z + k + 8, 8)
        return {"zh": t // 4, "zl": lax.rem(t, 4)}

    def start(src, dst, dev):
        i = count[0]
        count[0] += 1
        d = pltpu.make_async_remote_copy(
            src_ref=src, dst_ref=dst, send_sem=ss.at[i], recv_sem=rs.at[i],
            device_id=dev, device_id_type=MESH,
        )
        d.start()
        sends.append(d)
        return d

    def arrived(ds):
        for d in ds:
            d.wait_recv()

    ys = [other("y", k, 4) for k in (1, 3, 2)]
    xs = [other("x", k, 4) for k in (1, 3, 2)]
    sib = {"c": 1 - c}
    mpg = []
    for k in range(1, 8):
        m = lax.rem(zh * 4 + y + k, 8)
        mpg.append({"zh": m // 4, "y": lax.rem(m, 4)})
    xcg = []
    for k in range(1, 8):
        m = lax.rem(x * 2 + c + k, 8)
        xcg.append({"x": m // 2, "c": lax.rem(m, 2)})
    zlg = [other("zl", k, 4) for k in (1, 2, 3)]

    barrier = pltpu.get_barrier_semaphore()
    greet = mpg + xcg + zlg + [zto(1), zto(-1)]
    for d in greet:
        pl.semaphore_signal(barrier, 1, device_id=d, device_id_type=MESH)
    pl.semaphore_wait(barrier, len(greet))

    s0 = start(give, recv, sib)

    alpha = scal[0:1, 0:1]
    sigma = scal[1:2, 0:1]
    weight = scal[2:3, 0:1]
    noised[...] = (alpha * clean[...].astype(F32) + sigma * noise[...].astype(F32)).astype(BF)
    me = zh * 4 + y
    n1[me] = normed(noised[...], gains[0:1, :])
    tz = start(n1.at[me], n1.at[me], {"zh": 1 - zh})
    ty = [start(n1.at[me], n1.at[me], d) for d in ys]

    arrived([s0])
    mine = keep[...].astype(F32)
    theirs = recv[...].astype(F32)
    first = jnp.where(c == 0, mine, theirs)
    second = jnp.where(c == 0, theirs, mine)
    slab = jnp.concatenate([first, second], axis=0).astype(BF)
    qs[0] = slab[:, 0:128]
    qs[1] = slab[:, 128:256]
    w2[c, zh, zl, x] = slab[:, 896:1536]
    par = lax.rem(y, 2)
    ydst = 2 * zh + y // 2
    lane = pl.multiple_of(par * 128, 128)
    qsend = []
    base = count[0]
    count[0] += 2
    for h in range(2):
        here = jnp.logical_and(zh == h, y == ydst)
        dst = qw.at[c, h, zl, x, :, pl.ds(lane, 128)]
        away = pltpu.make_async_remote_copy(
            src_ref=qs.at[h], dst_ref=dst, send_sem=ss.at[base + h], recv_sem=rs.at[base + par],
            device_id={"zh": h, "y": ydst}, device_id_type=MESH,
        )
        local = pltpu.make_async_copy(qs.at[h], dst, ls)
        qsend.append((here, away, local))

        @pl.when(here)
        def _():
            local.start()

        @pl.when(jnp.logical_not(here))
        def _():
            away.start()

    @pl.when(c == 0)
    def _():
        wt[y] = slab[:, 256:512]

    @pl.when(c == 1)
    def _():
        w1[1, zh, zl, x] = slab[:, 256:896]

    wbase = count[0]
    count[0] += 3
    wy = [
        pltpu.make_async_remote_copy(
            src_ref=wt.at[y], dst_ref=wt.at[y], send_sem=ss.at[wbase + i],
            recv_sem=rs.at[wbase + i], device_id=d, device_id_type=MESH,
        )
        for i, d in enumerate(ys)
    ]

    @pl.when(c == 0)
    def _():
        for d in wy:
            d.start()

    def slab2(k):
        t = lax.rem(z + k + 8, 8)
        return t // 4, lax.rem(t, 4)

    own2 = w2.at[c, zh, zl, x]
    x2 = [start(own2, own2, d) for d in xs]

    homes = (jnp.logical_and(zh == 0, y == 0), jnp.logical_and(zh == 1, y == 3))
    alone = jnp.logical_or(*homes)
    for p in range(2):
        landed = pltpu.make_async_remote_copy(
            src_ref=qs.at[0], dst_ref=qw.at[c, zh, zl, x, :, pl.ds(p * 128, 128)],
            send_sem=ss.at[base], recv_sem=rs.at[base + p], device_id=sib, device_id_type=MESH,
        )
        self_slot = jnp.logical_and(alone, par == p)

        @pl.when(jnp.logical_not(self_slot))
        def _():
            landed.wait_recv()

    for here, away, local in qsend:

        @pl.when(here)
        def _():
            local.wait()

    def ring(ref, k, forward):
        a, b = slab2(-(k - 1) if forward else k - 1)
        return start(ref(a, b), ref(a, b), zto(1 if forward else -1))

    def q_ref(a, b):
        return qw.at[c, a, b, x]

    def w1_ref(a, b):
        return w1.at[c, a, b, x]

    def w2_ref(a, b):
        return w2.at[c, a, b]

    qf = ring(q_ref, 1, True)
    qb = ring(q_ref, 1, False)

    @pl.when(c == 0)
    def _():
        for d in wy:
            d.wait_recv()
        parts = [wt[j][:, 0:160].astype(F32) for j in range(4)]
        w1[0, zh, zl, x] = jnp.concatenate(parts, axis=1).astype(BF)

    x1 = []

    def spread1(k):
        r = w1_ref(*slab2(k))
        for d in xs:
            x1.append(start(r, r, d))

    f1 = ring(w1_ref, 1, True)
    b1 = ring(w1_ref, 1, False)
    spread1(0)

    arrived([qf, qb])
    qf = ring(q_ref, 2, True)
    qb = ring(q_ref, 2, False)
    arrived([qf, qb])
    qf = ring(q_ref, 3, True)
    qb = ring(q_ref, 3, False)
    arrived([f1, b1])
    f1 = ring(w1_ref, 2, True)
    b1 = ring(w1_ref, 2, False)
    spread1(-1)
    spread1(1)
    arrived([qf, qb])
    qf = ring(q_ref, 4, True)
    arrived([qf])
    xq = [start(qw.at[c, :, :, x], qw.at[c, :, :, x], d) for d in xs]

    arrived([f1, b1])
    f1 = ring(w1_ref, 3, True)
    b1 = ring(w1_ref, 3, False)
    spread1(-2)
    spread1(2)

    arrived([tz])
    far = (1 - zh) * 4 + y
    tfy = [start(n1.at[far], n1.at[far], d) for d in ys]

    arrived(x2)
    f2 = ring(w2_ref, 1, True)
    b2 = ring(w2_ref, 1, False)

    arrived([f1, b1])
    f1 = ring(w1_ref, 4, True)
    spread1(-3)
    spread1(3)

    arrived(xq)
    sq = start(qw.at[c], qw.at[c], sib)
    arrived(ty)
    arrived([sq])

    def project(half):
        rows = pl.ds(pl.multiple_of(half * 512, 512), 512)
        tokens = n1[pl.ds(half * 4, 4)].reshape(512, D)
        for t in range(4):
            w = qw[t // 2, t % 2].reshape(D, 256)
            out = jnp.dot(tokens, w, preferred_element_type=F32)
            qkv[t, rows] = out.astype(BF)

    project(zh)
    arrived([f1])
    spread1(-4)
    arrived([f2, b2])
    f2 = ring(w2_ref, 2, True)
    b2 = ring(w2_ref, 2, False)
    arrived(tfy)
    project(1 - zh)

    qrows = pl.multiple_of(zh * 512, 512)

    def pick(rows, spots):
        parts = [qkv[t, rows, a : a + n] for t, a, n in spots]
        if len(parts) == 1:
            return parts[0]
        return jnp.concatenate([p.astype(F32) for p in parts], axis=1).astype(BF)

    heads = (
        ([(0, 0, 64)], [(0, 64, 64)], [(2, 0, 64)]),
        ([(1, 0, 64)], [(1, 64, 64)], [(2, 64, 64)]),
        (
            [(3, 0, 32), (3, 128, 32)],
            [(3, 32, 32), (3, 160, 32)],
            [(3, 64, 32), (3, 192, 32)],
        ),
        ([(0, 128, 64)], [(0, 192, 64)], [(2, 128, 64)]),
        ([(1, 128, 64)], [(1, 192, 64)], [(2, 192, 64)]),
    )

    def attend(n):
        q_at, k_at, v_at = heads[n]
        keys = pick(pl.ds(0, L), k_at)
        values = pick(pl.ds(0, L), v_at)

        def tile(i, carry):
            r = pl.multiple_of(qrows + i * 128, 128)
            q = pick(pl.ds(r, 128), q_at) * BF(HEAD ** (-0.5))
            s = lax.dot_general(q, keys, NT, preferred_element_type=F32)
            p = jnp.exp(s - jnp.max(s, axis=1, keepdims=True))
            total = jnp.sum(p, axis=1, keepdims=True)
            o = jnp.dot(p.astype(BF), values, preferred_element_type=F32) / total
            mo[i, :, n * 64 : n * 64 + 64] = o.astype(BF)
            return carry

        lax.fori_loop(0, 4, tile, 0)

    attend(0)
    attend(1)
    arrived([f2, b2])
    f2 = ring(w2_ref, 3, True)
    b2 = ring(w2_ref, 3, False)
    attend(2)
    attend(3)
    attend(4)

    ax = []
    for k, d in zip((1, 3, 2), ys):
        to = lax.rem(y + k, 4)
        ax.append(start(mo.at[to], mx.at[y], d))
    mx[y] = mo[y]
    arrived([f2, b2])
    f2 = ring(w2_ref, 4, True)
    arrived(x1)
    s1 = start(w1.at[c], w1.at[c], sib)
    arrived(ax)
    arrived([s1])

    cols = []
    for h in range(2):
        acc = None
        for g in range(4):
            w = w1[0, h, g].reshape(320, 640)
            part = jnp.dot(mx[g][:, 0:320], w, preferred_element_type=F32)
            acc = part if acc is None else acc + part
        cols.append(acc)
    resid[...] = (noised[...].astype(F32) + jnp.concatenate(cols, axis=1)).astype(BF)
    n2[y] = normed(resid[...], gains[1:2, :])
    gy = [start(n2.at[y], n2.at[y], d) for d in ys]
    arrived([f2])
    s2 = start(w2.at[c], w2.at[c], sib)
    arrived(gy)
    arrived([s2])

    tokens = n2[...].reshape(512, D)
    for h in range(2):

        def hidden(i, carry):
            at = pl.ds(pl.multiple_of(i * 128, 128), 128)
            g = w2[0, h, :, :, :, at].reshape(D, 128)
            v = w1[1, h, :, :, :, at].reshape(D, 128)
            both = jnp.dot(
                tokens, jnp.concatenate([g, v], axis=1), preferred_element_type=F32
            )
            gate = both[:, 0:128]
            act = 0.5 * gate * (1.0 + lax.erf(gate * 0.5**0.5)) * both[:, 128:256]
            hid[h, :, at] = act.astype(BF)
            return carry

        lax.fori_loop(0, 5, hidden, 0)

    ry = []
    for n in range(5):
        acc = None
        for h in range(2):
            w = w2[1, h].reshape(D, 640)[n * 256 : n * 256 + 256]
            part = lax.dot_general(hid[h], w, NT, preferred_element_type=F32)
            acc = part if acc is None else acc + part
        fs[:, :, n * 256 : n * 256 + 256] = acc.astype(BF).reshape(4, ROWS, 256)
    for k, d in zip((1, 3, 2), ys):
        to = lax.rem(y + k, 4)
        ry.append(start(fs.at[to], ffin.at[y], d))
    ffin[y] = fs[y]
    arrived(ry)
    prediction = resid[...].astype(F32)
    for j in range(4):
        prediction = prediction + ffin[j].astype(F32)
    denoised = (noised[...].astype(F32) - sigma * prediction) / alpha
    den[0] = denoised
    error = denoised - clean[...].astype(F32)
    rowsum = jnp.sum(error * error, axis=1, keepdims=True)
    term = jnp.sum(rowsum, axis=0, keepdims=True) * weight

    def total(buf, slot, group, value):
        buf[slot] = jnp.broadcast_to(value, (8, 128))
        arrived([start(buf.at[slot], buf.at[slot], d) for d in group])
        out = buf[0]
        for j in range(1, len(group) + 1):
            out = out + buf[j]
        return out

    term = total(l1, me, mpg, term)
    term = total(l2, x * 2 + c, xcg, term)
    term = total(l3, zl, zlg, term)
    loss[...] = term

    for d in sends:
        d.wait_send()
    for here, away, local in qsend:

        @pl.when(jnp.logical_not(here))
        def _():
            away.wait_send()

    @pl.when(c == 0)
    def _():
        for d in wy:
            d.wait_send()


N_COPIES = 112


def shards(
    clean, noise, tsteps, alpha_tab, weight_tab, norm1_gain, norm2_gain,
    wqkv, wout, wgate, wvalue, wdown,
):
    alpha = lookup(tsteps, alpha_tab)
    sigma = jnp.sqrt(1.0 - alpha * alpha)
    weight = lookup(tsteps, weight_tab) / (L * D)
    scal = jnp.concatenate([alpha, sigma, weight, jnp.zeros((5,), F32)])
    scal = jnp.broadcast_to(scal[:, None], (8, 128))
    gains = jnp.stack([norm1_gain, norm2_gain])

    even = lax.rem(lax.axis_index("y"), 2) == 0
    first = lax.axis_index("c") == 0
    h_a = jnp.where(even, wqkv[:, :, 0:64], wqkv[:, :, 32:96])
    h_b = jnp.where(even, wqkv[:, :, 64:128], wqkv[:, :, 96:160])
    h_s = jnp.where(even, wqkv[:, :, 128:160], wqkv[:, :, 0:32])
    rows = wout.shape[0]
    t0 = [h_a[0], h_a[1]]
    t1 = [h_b[0], h_b[1]]
    t2 = [h_a[2], h_b[2]]
    t3 = [h_s[0], h_s[1], h_s[2], jnp.zeros((rows, 32), BF)]
    pad = jnp.zeros((rows, 480), BF)
    for_0 = jnp.concatenate(t0 + t1 + [wout, pad, wgate], axis=1)
    for_1 = jnp.concatenate(t2 + t3 + [wvalue, wdown.T], axis=1)
    keep = jnp.where(first, for_0, for_1)
    give = jnp.where(first, for_1, for_0)

    vm = pl.BlockSpec(memory_space=pltpu.VMEM)
    den, loss = pl.pallas_call(
        kernel,
        out_shape=(
            jax.ShapeDtypeStruct((1, ROWS, D), F32),
            jax.ShapeDtypeStruct((8, 128), F32),
        ),
        in_specs=[vm] * 6,
        out_specs=(vm, vm),
        scratch_shapes=[
            pltpu.VMEM((40, 1536), BF),
            pltpu.VMEM((2, 80, 128), BF),
            pltpu.VMEM((4, 80, 256), BF),
            pltpu.VMEM((2, 2, 4, 4, 80, 256), BF),
            pltpu.VMEM((2, 2, 4, 4, 80, 640), BF),
            pltpu.VMEM((2, 2, 4, 4, 80, 640), BF),
            pltpu.VMEM((8, ROWS, D), BF),
            pltpu.VMEM((4, L, 256), BF),
            pltpu.VMEM((4, ROWS, 384), BF),
            pltpu.VMEM((4, ROWS, 384), BF),
            pltpu.VMEM((4, ROWS, D), BF),
            pltpu.VMEM((2, 512, 640), BF),
            pltpu.VMEM((4, ROWS, D), BF),
            pltpu.VMEM((4, ROWS, D), BF),
            pltpu.VMEM((ROWS, D), BF),
            pltpu.VMEM((ROWS, D), BF),
            pltpu.VMEM((8, 8, 128), F32),
            pltpu.VMEM((8, 8, 128), F32),
            pltpu.VMEM((4, 8, 128), F32),
            pltpu.SemaphoreType.DMA((N_COPIES,)),
            pltpu.SemaphoreType.DMA((N_COPIES,)),
            pltpu.SemaphoreType.DMA,
        ],
        compiler_params=pltpu.CompilerParams(
            collective_id=0, has_side_effects=True, vmem_limit_bytes=60 * 2**20
        ),
    )(clean[0], noise[0], scal, gains, keep, give)
    return den, loss[0, 0]


def solution(mesh):
    split = Mesh(mesh.devices.reshape(4, 4, 2, 2, 4), AXES)
    in_specs = (
        P(DP, MP, None), P(DP, MP, None), P(DP), P(), P(), P(), P(),
        P(None, DP, MP), P(DP, MP), P(DP, MP), P(DP, MP), P(MP, DP),
    )
    out_specs = (P(DP, MP, None), P())
    return jax.shard_map(
        shards, mesh=split, in_specs=in_specs, out_specs=out_specs, check_vma=False
    )
```

```python
import jax
import jax.numpy as jnp
from jax import lax
from jax.experimental import pallas as pl
from jax.experimental.pallas import tpu as pltpu
from jax.sharding import Mesh
from jax.sharding import PartitionSpec as P

D = 1280
HEAD = 64
L = 1024
ROWS = 128
AXES = ("zl", "x", "c", "zh", "y")
DP = ("zl", "x", "c")
MP = ("zh", "y")
MESH = pl.DeviceIdType.MESH
BF = jnp.bfloat16
F32 = jnp.float32
NT = (((1,), (1,)), ((), ()))


def normed(values, gain):
    wide = values.astype(F32)
    center = wide - jnp.mean(wide, axis=-1, keepdims=True)
    spread = jnp.mean(center * center, axis=-1, keepdims=True)
    return (center * lax.rsqrt(spread + 1e-05) * gain).astype(BF)


def kernel(
    tsteps, clean, noise, alpha_tab, weight_tab, gain1, gain2, wqkv, wout, wgate, wvalue, wdown,
    den, loss,
    keep, give, recv, qs, wt, qw, w1, w2, n1, qh, kh, vh, mo, mx, n2, hid, fs, ffin, noised, resid,
    l1, l2, ss, rs, ls,
):
    zl, x, c, zh, y = (lax.axis_index(a) for a in AXES)
    z = zh * 4 + zl
    sends = []
    count = [0]

    def other(name, k, n):
        return {name: lax.rem(lax.axis_index(name) + k, n)}

    def zto(k):
        t = lax.rem(z + k + 8, 8)
        return {"zh": t // 4, "zl": lax.rem(t, 4)}

    def make(src, dst, dev):
        i = count[0]
        count[0] += 1
        d = pltpu.make_async_remote_copy(
            src_ref=src, dst_ref=dst, send_sem=ss.at[i], recv_sem=rs.at[i],
            device_id=dev, device_id_type=MESH,
        )
        sends.append(d)
        return d

    def start(src, dst, dev):
        d = make(src, dst, dev)
        d.start()
        return d

    def arrived(ds):
        for d in ds:
            d.wait_recv()

    ys = [other("y", k, 4) for k in (1, 3, 2)]
    xs = [other("x", k, 4) for k in (1, 3, 2)]
    sib = {"c": 1 - c}
    plane = []
    for k in range(1, 16):
        m = lax.rem(x * 4 + y + k, 16)
        plane.append({"x": m // 4, "y": lax.rem(m, 4)})
    column = []
    for k in range(1, 16):
        m = lax.rem(z * 2 + c + k, 16)
        column.append({"zh": m // 8, "zl": lax.rem(m // 2, 4), "c": lax.rem(m, 2)})
    across = [{"zh": 1 - zh, "y": lax.rem(y + k, 4)} for k in (1, 2, 3)]

    barrier = pltpu.get_barrier_semaphore()
    greet = plane + column + across
    for d in greet:
        pl.semaphore_signal(barrier, 1, device_id=d, device_id_type=MESH)

    step = tsteps[0]
    match = lax.broadcasted_iota(jnp.int32, alpha_tab.shape, 1) == step
    alpha = jnp.sum(jnp.where(match, alpha_tab[...], 0.0), axis=1, keepdims=True)
    weight = jnp.sum(jnp.where(match, weight_tab[...], 0.0), axis=1, keepdims=True) / (L * D)
    sigma = jnp.sqrt(1.0 - alpha * alpha)

    par = lax.rem(y, 2)

    def fold(value, mine_at):
        value = value.astype(BF)
        at = pl.ds(mine_at[1], value.shape[1])

        @pl.when(c == mine_at[0])
        def _():
            keep[:, at] = value

        @pl.when(c != mine_at[0])
        def _():
            give[:, at] = value

    wide = [wqkv[j].astype(F32) for j in range(3)]
    h_a = [jnp.where(par == 0, w[:, 0:64], w[:, 32:96]) for w in wide]
    h_b = [jnp.where(par == 0, w[:, 64:128], w[:, 96:160]) for w in wide]
    h_s = [jnp.where(par == 0, w[:, 128:160], w[:, 0:32]) for w in wide]
    fold(jnp.concatenate([h_a[0], h_a[1]], axis=1), (0, 0))
    fold(jnp.concatenate([h_b[0], h_b[1]], axis=1), (0, 128))
    fold(jnp.concatenate([h_a[2], h_b[2]], axis=1), (1, 0))
    fold(jnp.concatenate(h_s + [jnp.zeros((40, 32), F32)], axis=1), (1, 128))
    fold(jnp.concatenate([wout[...].astype(F32), jnp.zeros((40, 96), F32)], axis=1), (0, 256))
    fold(wvalue[...], (1, 256))
    fold(wgate[...], (0, 896))
    fold(wdown[...].astype(F32).T, (1, 896))

    noised[...] = (alpha * clean[...].astype(F32) + sigma * noise[...].astype(F32)).astype(BF)
    me = zh * 4 + y
    n1[me] = normed(noised[...], gain1[...])

    pl.semaphore_wait(barrier, len(greet))
    s0 = start(give, recv, sib)
    tz = start(n1.at[me], n1.at[me], {"zh": 1 - zh})

    def spread_y(ref):
        return [start(ref(y), ref(y), d) for d in ys[:2]]

    def relay_y(ref):
        low, high = pl.ds(0, 64), pl.ds(64, 64)
        a, b = ref(lax.rem(y + 3, 4)).at[low], ref(lax.rem(y + 1, 4)).at[high]
        return [start(a, a, ys[0]), start(b, b, ys[1])]

    def near(j):
        return n1.at[zh * 4 + j]

    def far(j):
        return n1.at[(1 - zh) * 4 + j]

    ty = spread_y(near)

    arrived([s0])
    mine = keep[...].astype(F32)
    theirs = recv[...].astype(F32)
    first = jnp.where(c == 0, mine, theirs)
    second = jnp.where(c == 0, theirs, mine)
    slab = jnp.concatenate([first, second], axis=0).astype(BF)
    qs[0] = slab[:, 0:128]
    qs[1] = slab[:, 128:256]
    w2[c, zh, zl, x] = slab[:, 896:1536]
    ydst = 2 * zh + y // 2
    lane = pl.multiple_of(par * 128, 128)
    qsend = []
    base = count[0]
    count[0] += 2
    for h in range(2):
        here = jnp.logical_and(zh == h, y == ydst)
        dst = qw.at[c, h, zl, x, :, pl.ds(lane, 128)]
        away = pltpu.make_async_remote_copy(
            src_ref=qs.at[h], dst_ref=dst, send_sem=ss.at[base + h], recv_sem=rs.at[base + par],
            device_id={"zh": h, "y": ydst}, device_id_type=MESH,
        )
        local = pltpu.make_async_copy(qs.at[h], dst, ls)
        qsend.append((here, away, local))

        @pl.when(here)
        def _():
            local.start()

        @pl.when(jnp.logical_not(here))
        def _():
            away.start()

    @pl.when(c == 0)
    def _():
        wt[y] = slab[:, 256:512]

    @pl.when(c == 1)
    def _():
        w1[1, zh, zl, x] = slab[:, 256:896]

    wbase = count[0]
    count[0] += 3
    wy = [
        pltpu.make_async_remote_copy(
            src_ref=wt.at[y], dst_ref=wt.at[y], send_sem=ss.at[wbase + i],
            recv_sem=rs.at[wbase + i], device_id=d, device_id_type=MESH,
        )
        for i, d in enumerate(ys)
    ]

    @pl.when(c == 0)
    def _():
        for d in wy:
            d.start()

    def slab2(k):
        t = lax.rem(z + k + 8, 8)
        return t // 4, lax.rem(t, 4)

    own2 = w2.at[c, zh, zl, x]
    x2 = [start(own2, own2, d) for d in xs]

    homes = (jnp.logical_and(zh == 0, y == 0), jnp.logical_and(zh == 1, y == 3))
    alone = jnp.logical_or(*homes)
    for p in range(2):
        landed = pltpu.make_async_remote_copy(
            src_ref=qs.at[0], dst_ref=qw.at[c, zh, zl, x, :, pl.ds(p * 128, 128)],
            send_sem=ss.at[base], recv_sem=rs.at[base + p], device_id=sib, device_id_type=MESH,
        )
        self_slot = jnp.logical_and(alone, par == p)

        @pl.when(jnp.logical_not(self_slot))
        def _():
            landed.wait_recv()

    for here, away, local in qsend:

        @pl.when(here)
        def _():
            local.wait()

    def hop(ref, k, forward):
        a, b = slab2(-(k - 1) if forward else k - 1)
        return make(ref(a, b), ref(a, b), zto(1 if forward else -1))

    def ring(ref, k, forward):
        d = hop(ref, k, forward)
        d.start()
        return d

    def q_ref(a, b):
        return qw.at[c, a, b, x]

    def w1_ref(a, b):
        return w1.at[c, a, b, x]

    def w2_ref(a, b):
        return w2.at[c, a, b]

    qf = ring(q_ref, 1, True)
    qb = ring(q_ref, 1, False)

    @pl.when(c == 0)
    def _():
        for d in wy:
            d.wait_recv()
        parts = [wt[j][:, 0:160].astype(F32) for j in range(4)]
        w1[0, zh, zl, x] = jnp.concatenate(parts, axis=1).astype(BF)

    x1 = []

    def spread1(k):
        r = w1_ref(*slab2(k))
        for d in xs:
            x1.append(start(r, r, d))

    f1 = ring(w1_ref, 1, True)
    b1 = ring(w1_ref, 1, False)
    spread1(0)

    arrived([qf, qb])
    qf = ring(q_ref, 2, True)
    qb = ring(q_ref, 2, False)
    arrived(ty)
    ty = relay_y(near)
    arrived([qf, qb])
    qf = ring(q_ref, 3, True)
    qb = ring(q_ref, 3, False)
    arrived([f1, b1])
    f1 = ring(w1_ref, 2, True)
    b1 = ring(w1_ref, 2, False)
    spread1(-1)
    spread1(1)
    arrived([qf, qb])
    qf = ring(q_ref, 4, True)
    arrived([qf])
    xq = [start(qw.at[c, :, :, x], qw.at[c, :, :, x], d) for d in xs]
    arrived([tz])
    tf = spread_y(far)

    arrived([f1, b1])
    f1 = ring(w1_ref, 3, True)
    b1 = ring(w1_ref, 3, False)
    spread1(-2)
    spread1(2)

    arrived(x2)
    f2 = ring(w2_ref, 1, True)
    b2 = ring(w2_ref, 1, False)

    arrived(xq)
    sq = start(qw.at[c], qw.at[c], sib)
    arrived(ty)
    arrived(tf)
    tf = relay_y(far)

    arrived([f1, b1])
    f1 = ring(w1_ref, 4, True)
    spread1(-3)
    spread1(3)
    arrived([sq])

    def project(half):
        rows = pl.ds(pl.multiple_of(half * 512, 512), 512)
        tokens = n1[pl.ds(half * 4, 4)].reshape(512, D)

        def out(t):
            w = qw[t // 2, t % 2].reshape(D, 256)
            return jnp.dot(tokens, w, preferred_element_type=F32)

        def put(ref, n, value):
            ref[n, rows] = value.astype(BF)

        for t, heads in ((0, (0, 3)), (1, (1, 4))):
            o = out(t)
            for j, n in enumerate(heads):
                put(qh, n, o[:, j * 128 : j * 128 + 64] * HEAD ** (-0.5))
                put(kh, n, o[:, j * 128 + 64 : j * 128 + 128])
        o = out(2)
        for j, n in enumerate((0, 1, 3, 4)):
            put(vh, n, o[:, j * 64 : j * 64 + 64])
        o = out(3)
        halves = [
            jnp.concatenate([o[:, j : j + 32], o[:, j + 128 : j + 160]], axis=1)
            for j in (0, 32, 64)
        ]
        put(qh, 2, halves[0] * HEAD ** (-0.5))
        put(kh, 2, halves[1])
        put(vh, 2, halves[2])

    project(zh)
    arrived([f1])
    spread1(-4)
    arrived([f2, b2])
    f2 = ring(w2_ref, 2, True)
    b2 = ring(w2_ref, 2, False)
    arrived(tf)
    project(1 - zh)

    held = [f2, b2]
    f2 = hop(w2_ref, 3, True)
    b2 = hop(w2_ref, 3, False)
    abase = count[0]
    count[0] += 3

    def give_tile(t, i):
        return pltpu.make_async_remote_copy(
            src_ref=mo.at[i], dst_ref=mx.at[y], send_sem=ss.at[abase + t],
            recv_sem=rs.at[abase + t], device_id={"y": i}, device_id_type=MESH,
        )

    def attend(t, carry):
        i = lax.rem(y + t + 1, 4)
        r = pl.ds(pl.multiple_of(zh * 512 + i * 128, 128), 128)

        @pl.when(t == 2)
        def _():
            arrived(held)
            f2.start()
            b2.start()

        for n in range(5):
            s = lax.dot_general(qh[n, r], kh[n], NT, preferred_element_type=F32)
            p = jnp.exp(s - jnp.max(s, axis=1, keepdims=True))
            total = jnp.sum(p, axis=1, keepdims=True)
            o = jnp.dot(p.astype(BF), vh[n], preferred_element_type=F32) / total
            mo[i, :, n * 64 : n * 64 + 64] = o.astype(BF)

        @pl.when(t < 3)
        def _():
            give_tile(t, i).start()

        return carry

    lax.fori_loop(0, 4, attend, 0)
    ax = [give_tile(t, lax.rem(y + t + 1, 4)) for t in range(3)]
    sends.extend(ax)

    arrived([f2, b2])
    f2 = ring(w2_ref, 4, True)
    arrived(x1)
    s1 = start(w1.at[c], w1.at[c], sib)
    mx[y] = mo[y]
    arrived(ax)
    arrived([s1])

    cols = []
    for h in range(2):
        acc = None
        for g in range(4):
            w = w1[0, h, g].reshape(320, 640)
            part = jnp.dot(mx[g][:, 0:320], w, preferred_element_type=F32)
            acc = part if acc is None else acc + part
        cols.append(acc)
    resid[...] = (noised[...].astype(F32) + jnp.concatenate(cols, axis=1)).astype(BF)
    n2[y] = normed(resid[...], gain2[...])

    def block(j):
        return n2.at[j]

    gy = spread_y(block)
    arrived([f2])
    s2 = start(w2.at[c], w2.at[c], sib)
    arrived([s2])

    def feed(blocks, ship):
        m = ROWS * len(blocks)
        tokens = jnp.concatenate([n2[j] for j in blocks], axis=0) if m > ROWS else n2[blocks[0]]
        for h in range(2):

            def hidden(i, carry):
                at = pl.ds(pl.multiple_of(i * 128, 128), 128)
                g = w2[0, h, :, :, :, at].reshape(D, 128)
                v = w1[1, h, :, :, :, at].reshape(D, 128)
                both = jnp.dot(
                    tokens, jnp.concatenate([g, v], axis=1), preferred_element_type=F32
                )
                gate = both[:, 0:128]
                act = 0.5 * gate * (1.0 + lax.erf(gate * 0.5**0.5)) * both[:, 128:256]
                hid[h, 0:m, at] = act.astype(BF)
                return carry

            lax.fori_loop(0, 5, hidden, 0)
        copies = []
        for n in range(5):
            acc = None
            for h in range(2):
                w = w2[1, h].reshape(D, 640)[n * 256 : n * 256 + 256]
                part = lax.dot_general(hid[h, 0:m], w, NT, preferred_element_type=F32)
                acc = part if acc is None else acc + part
            at = pl.ds(n * 256, 256)
            for q, j in enumerate(blocks):
                part = acc[q * ROWS : q * ROWS + ROWS].astype(BF)
                if ship:
                    fs[j, :, at] = part
                    copies.append(start(fs.at[j, :, at], ffin.at[y, :, at], {"y": j}))
                else:
                    ffin[j, :, at] = part
        return copies

    feed([y], False)
    arrived(gy)
    gy = relay_y(block)
    ry = feed([lax.rem(y + 1, 4), lax.rem(y + 3, 4)], True)
    arrived(gy)
    ry += feed([lax.rem(y + 2, 4)], True)
    arrived(ry)
    prediction = resid[...].astype(F32)
    for j in range(4):
        prediction = prediction + ffin[j].astype(F32)
    denoised = (noised[...].astype(F32) - sigma * prediction) / alpha
    den[0] = denoised
    error = denoised - clean[...].astype(F32)
    rowsum = jnp.sum(error * error, axis=1, keepdims=True)
    term = jnp.sum(rowsum, axis=0, keepdims=True) * weight

    def total(buf, slot, group, value):
        buf[slot] = jnp.broadcast_to(value, (8, 128))
        arrived([start(buf.at[slot], buf.at[slot], d) for d in group])
        out = buf[0]
        for j in range(1, len(group) + 1):
            out = out + buf[j]
        return out

    term = total(l1, x * 4 + y, plane, term)
    term = total(l2, z * 2 + c, column, term)
    loss[...] = term

    for d in sends:
        d.wait_send()
    for here, away, local in qsend:

        @pl.when(jnp.logical_not(here))
        def _():
            away.wait_send()

    @pl.when(c == 0)
    def _():
        for d in wy:
            d.wait_send()


N_COPIES = 144


def shards(
    clean, noise, tsteps, alpha_tab, weight_tab, norm1_gain, norm2_gain,
    wqkv, wout, wgate, wvalue, wdown,
):
    vm = pl.BlockSpec(memory_space=pltpu.VMEM)
    den, loss = pl.pallas_call(
        kernel,
        out_shape=(
            jax.ShapeDtypeStruct((1, ROWS, D), F32),
            jax.ShapeDtypeStruct((8, 128), F32),
        ),
        in_specs=[pl.BlockSpec(memory_space=pltpu.SMEM)] + [vm] * 11,
        out_specs=(vm, vm),
        scratch_shapes=[
            pltpu.VMEM((40, 1536), BF),
            pltpu.VMEM((40, 1536), BF),
            pltpu.VMEM((40, 1536), BF),
            pltpu.VMEM((2, 80, 128), BF),
            pltpu.VMEM((4, 80, 256), BF),
            pltpu.VMEM((2, 2, 4, 4, 80, 256), BF),
            pltpu.VMEM((2, 2, 4, 4, 80, 640), BF),
            pltpu.VMEM((2, 2, 4, 4, 80, 640), BF),
            pltpu.VMEM((8, ROWS, D), BF),
            pltpu.VMEM((5, L, 64), BF),
            pltpu.VMEM((5, L, 64), BF),
            pltpu.VMEM((5, L, 64), BF),
            pltpu.VMEM((4, ROWS, 384), BF),
            pltpu.VMEM((4, ROWS, 384), BF),
            pltpu.VMEM((4, ROWS, D), BF),
            pltpu.VMEM((2, 256, 640), BF),
            pltpu.VMEM((4, ROWS, D), BF),
            pltpu.VMEM((4, ROWS, D), BF),
            pltpu.VMEM((ROWS, D), BF),
            pltpu.VMEM((ROWS, D), BF),
            pltpu.VMEM((16, 8, 128), F32),
            pltpu.VMEM((16, 8, 128), F32),
            pltpu.SemaphoreType.DMA((N_COPIES,)),
            pltpu.SemaphoreType.DMA((N_COPIES,)),
            pltpu.SemaphoreType.DMA,
        ],
        compiler_params=pltpu.CompilerParams(
            collective_id=0, has_side_effects=True, vmem_limit_bytes=60 * 2**20
        ),
    )(
        tsteps, clean[0], noise[0], alpha_tab[None], weight_tab[None], norm1_gain[None],
        norm2_gain[None], wqkv, wout, wgate, wvalue, wdown,
    )
    return den, loss[0, 0]


def solution(mesh):
    split = Mesh(mesh.devices.reshape(4, 4, 2, 2, 4), AXES)
    in_specs = (
        P(DP, MP, None), P(DP, MP, None), P(DP), P(), P(), P(), P(),
        P(None, DP, MP), P(DP, MP), P(DP, MP), P(DP, MP), P(MP, DP),
    )
    out_specs = (P(DP, MP, None), P())
    return jax.shard_map(
        shards, mesh=split, in_specs=in_specs, out_specs=out_specs, check_vma=False
    )
```

```python
import jax
import jax.numpy as jnp
from jax import lax
from jax.experimental import pallas as pl
from jax.experimental.pallas import tpu as pltpu
from jax.sharding import Mesh
from jax.sharding import PartitionSpec as P

D = 1280
HEAD = 64
L = 1024
ROWS = 128
AXES = ("zl", "x", "c", "zh", "y")
DP = ("zl", "x", "c")
MP = ("zh", "y")
MESH = pl.DeviceIdType.MESH
BF = jnp.bfloat16
F32 = jnp.float32
NT = (((1,), (1,)), ((), ()))


def normed(values, gain):
    wide = values.astype(F32)
    center = wide - jnp.mean(wide, axis=-1, keepdims=True)
    spread = jnp.mean(center * center, axis=-1, keepdims=True)
    return (center * lax.rsqrt(spread + 1e-05) * gain).astype(BF)


def kernel(
    tsteps, clean, noise, alpha_tab, weight_tab, gain1, gain2, wqkv, wout, wgate, wvalue, wdown,
    den, loss,
    keep, give, recv, qs, wt, qw, wb, n1, qh, kh, vh, mo, mx, n2, hid, fs, ffin, noised, resid,
    l1, l2, ss, rs, ls,
):
    zl, x, c, zh, y = (lax.axis_index(a) for a in AXES)
    z = zh * 4 + zl
    sends = []
    count = [0]

    def other(name, k, n):
        return {name: lax.rem(lax.axis_index(name) + k, n)}

    def zto(k):
        t = lax.rem(z + k + 8, 8)
        return {"zh": t // 4, "zl": lax.rem(t, 4)}

    def make(src, dst, dev):
        i = count[0]
        count[0] += 1
        d = pltpu.make_async_remote_copy(
            src_ref=src, dst_ref=dst, send_sem=ss.at[i], recv_sem=rs.at[i],
            device_id=dev, device_id_type=MESH,
        )
        sends.append(d)
        return d

    def start(src, dst, dev):
        d = make(src, dst, dev)
        d.start()
        return d

    def arrived(ds):
        for d in ds:
            d.wait_recv()

    ys = [other("y", k, 4) for k in (1, 3, 2)]
    xs = [other("x", k, 4) for k in (1, 3, 2)]
    sib = {"c": 1 - c}
    plane = []
    for k in range(1, 16):
        m = lax.rem(x * 4 + y + k, 16)
        plane.append({"x": m // 4, "y": lax.rem(m, 4)})
    column = []
    for k in range(1, 16):
        m = lax.rem(z * 2 + c + k, 16)
        column.append({"zh": m // 8, "zl": lax.rem(m // 2, 4), "c": lax.rem(m, 2)})
    across = [{"zh": 1 - zh, "y": lax.rem(y + k, 4)} for k in (1, 2, 3)]

    barrier = pltpu.get_barrier_semaphore()
    greet = plane + column + across
    for d in greet:
        pl.semaphore_signal(barrier, 1, device_id=d, device_id_type=MESH)

    step = tsteps[0]
    match = lax.broadcasted_iota(jnp.int32, alpha_tab.shape, 1) == step
    alpha = jnp.sum(jnp.where(match, alpha_tab[...], 0.0), axis=1, keepdims=True)
    weight = jnp.sum(jnp.where(match, weight_tab[...], 0.0), axis=1, keepdims=True) / (L * D)
    sigma = jnp.sqrt(1.0 - alpha * alpha)

    par = lax.rem(y, 2)

    def fold(value, mine_at):
        value = value.astype(BF)
        at = pl.ds(mine_at[1], value.shape[1])

        @pl.when(c == mine_at[0])
        def _():
            keep[:, at] = value

        @pl.when(c != mine_at[0])
        def _():
            give[:, at] = value

    wide = [wqkv[j].astype(F32) for j in range(3)]
    h_a = [jnp.where(par == 0, w[:, 0:64], w[:, 32:96]) for w in wide]
    h_b = [jnp.where(par == 0, w[:, 64:128], w[:, 96:160]) for w in wide]
    h_s = [jnp.where(par == 0, w[:, 128:160], w[:, 0:32]) for w in wide]
    fold(jnp.concatenate([h_a[0], h_a[1]], axis=1), (0, 0))
    fold(jnp.concatenate([h_b[0], h_b[1]], axis=1), (0, 128))
    fold(jnp.concatenate([h_a[2], h_b[2]], axis=1), (1, 0))
    fold(jnp.concatenate(h_s + [jnp.zeros((40, 32), F32)], axis=1), (1, 128))
    fold(jnp.concatenate([wout[...].astype(F32), jnp.zeros((40, 96), F32)], axis=1), (0, 256))
    fold(wvalue[...], (1, 256))
    fold(wgate[...], (0, 896))
    fold(wdown[...], (1, 896))

    noised[...] = (alpha * clean[...].astype(F32) + sigma * noise[...].astype(F32)).astype(BF)
    me = zh * 4 + y
    n1[me] = normed(noised[...], gain1[...])

    pl.semaphore_wait(barrier, len(greet))
    s0 = start(give, recv, sib)

    def spread_y(ref):
        return [start(ref(y), ref(y), d) for d in ys[:2]]

    def relay_y(ref):
        low, high = pl.ds(0, 64), pl.ds(64, 64)
        a, b = ref(lax.rem(y + 3, 4)).at[low], ref(lax.rem(y + 1, 4)).at[high]
        return [start(a, a, ys[0]), start(b, b, ys[1])]

    def near(j):
        return n1.at[zh * 4 + j]

    def far(j):
        return n1.at[(1 - zh) * 4 + j]

    arrived([s0])
    mine = keep[...].astype(F32)
    theirs = recv[...].astype(F32)
    first = jnp.where(c == 0, mine, theirs)
    second = jnp.where(c == 0, theirs, mine)
    slab = jnp.concatenate([first, second], axis=0).astype(BF)
    qs[0] = slab[:, 0:128]
    qs[1] = slab[:, 128:256]
    wb[c, zh, zl, x, :, 640:1280] = slab[:, 896:1536]
    ydst = 2 * zh + y // 2
    lane = pl.multiple_of(par * 128, 128)
    qsend = []
    base = count[0]
    count[0] += 2
    for h in range(2):
        here = jnp.logical_and(zh == h, y == ydst)
        dst = qw.at[c, h, zl, x, :, pl.ds(lane, 128)]
        away = pltpu.make_async_remote_copy(
            src_ref=qs.at[h], dst_ref=dst, send_sem=ss.at[base + h], recv_sem=rs.at[base + par],
            device_id={"zh": h, "y": ydst}, device_id_type=MESH,
        )
        local = pltpu.make_async_copy(qs.at[h], dst, ls)
        qsend.append((here, away, local))

        @pl.when(here)
        def _():
            local.start()

        @pl.when(jnp.logical_not(here))
        def _():
            away.start()

    @pl.when(c == 0)
    def _():
        wt[y] = slab[:, 256:512]

    @pl.when(c == 1)
    def _():
        wb[1, zh, zl, x, :, 0:640] = slab[:, 256:896]

    wbase = count[0]
    count[0] += 3
    wy = [
        pltpu.make_async_remote_copy(
            src_ref=wt.at[y], dst_ref=wt.at[y], send_sem=ss.at[wbase + i],
            recv_sem=rs.at[wbase + i], device_id=d, device_id_type=MESH,
        )
        for i, d in enumerate(ys)
    ]

    @pl.when(c == 0)
    def _():
        for d in wy:
            d.start()

    def slab2(k):
        t = lax.rem(z + k + 8, 8)
        return t // 4, lax.rem(t, 4)

    own2 = wb.at[c, zh, zl, x, :, CUT:1280]
    x2 = [start(own2, own2, d) for d in xs]
    ty = spread_y(near)
    tz = []

    def cross(*ks):
        for k in ks:
            r = n1.at[me, pl.ds(32 * k, 32)]
            tz.append(start(r, r, {"zh": 1 - zh}))

    cross(0)

    @pl.when(c == 0)
    def _():
        for d in wy:
            d.wait_recv()
        parts = [wt[j][:, 0:160].astype(F32) for j in range(4)]
        wb[0, zh, zl, x, :, 0:640] = jnp.concatenate(parts, axis=1).astype(BF)

    def hop(ref, k, forward):
        a, b = slab2(-(k - 1) if forward else k - 1)
        r = ref(a, b, None if k < 4 else 1 - int(forward))
        return make(r, r, zto(1 if forward else -1))

    def ring(ref, k):
        ds = [hop(ref, k, True), hop(ref, k, False)]
        for d in ds:
            d.start()
        return ds

    def even_ref(a, b, part):
        rows = slice(None) if part is None else slice(48 * part, 48 + 32 * part)
        return qw.at[c, a, b, x, rows, 0:128]

    def odd_ref(a, b, part):
        which = slice(None) if part is None else slice(2 * part, 2 * part + 2)
        return qw.at[c, a, b, which, :, 128:256]

    def w1_ref(a, b, part):
        cols = slice(0, CUT) if part is None else slice(CUT // 2 * part, CUT // 2 * (part + 1))
        return wb.at[c, a, b, x, :, cols]

    def w2_ref(a, b, part):
        which = slice(None) if part is None else slice(2 * part, 2 * part + 2)
        return wb.at[c, a, b, which, :, CUT:1280]

    x1 = {}

    def spread1(*ks):
        for k in ks:
            r = w1_ref(*slab2(k), None)
            x1[k] = [start(r, r, d) for d in xs[:2]]

    x1b = []

    def relay1(*ks):
        for k in ks:
            arrived(x1[k])
            a, b = slab2(k)
            turn = 1 + 2 * a
            r = wb.at[c, a, b, lax.rem(x + 4 - turn, 4), :, 0:CUT]
            x1b.append(start(r, r, {"x": lax.rem(x + turn, 4)}))

    spread1(0)

    homes = (jnp.logical_and(zh == 0, y == 0), jnp.logical_and(zh == 1, y == 3))
    alone = jnp.logical_or(*homes)
    for p in range(2):
        landed = pltpu.make_async_remote_copy(
            src_ref=qs.at[0], dst_ref=qw.at[c, zh, zl, x, :, pl.ds(p * 128, 128)],
            send_sem=ss.at[base], recv_sem=rs.at[base + p], device_id=sib, device_id_type=MESH,
        )
        self_slot = jnp.logical_and(alone, par == p)

        @pl.when(jnp.logical_not(self_slot))
        def _():
            landed.wait_recv()

    for here, away, local in qsend:

        @pl.when(here)
        def _():
            local.wait()

    er = ring(even_ref, 1)
    cross(1)
    odd = qw.at[c, zh, zl, x, :, 128:256]
    ox = [start(odd, odd, d) for d in xs]

    arrived(er)
    er = ring(even_ref, 2)
    w1r = ring(w1_ref, 1)
    arrived(ox)
    dr = ring(odd_ref, 1)
    arrived(er)
    er = ring(even_ref, 3)
    cross(2)
    arrived(dr)
    dr = ring(odd_ref, 2)
    arrived(er)
    er = ring(even_ref, 4)
    cross(3)
    arrived(w1r)
    spread1(-1, 1)
    arrived(ty)
    ty = relay_y(near)
    arrived(er)
    ex = [
        start(qw.at[c, :, :, x, :, 0:128], qw.at[c, :, :, x, :, 0:128], d) for d in xs
    ]
    arrived(dr)
    dr = ring(odd_ref, 3)
    w1r = ring(w1_ref, 2)
    relay1(0)
    arrived(tz)
    tf = spread_y(far)
    arrived(dr)
    dr = ring(odd_ref, 4)
    arrived(w1r)
    w1r = ring(w1_ref, 3)
    spread1(-2, 2)
    arrived(ex)
    half = qw.at[c, :, :, :, :, 0:128]
    sq = [start(half, half, sib)]
    arrived(dr)
    half = qw.at[c, :, :, :, :, 128:256]
    sq.append(start(half, half, sib))
    relay1(-1, 1)
    arrived(x2)
    w2r = ring(w2_ref, 1)
    arrived(tf)
    tf = relay_y(far)
    arrived(w1r)
    w1r = ring(w1_ref, 4)
    spread1(-3, 3)
    arrived(ty)
    arrived(sq)

    def project(half):
        rows = pl.ds(pl.multiple_of(half * 512, 512), 512)
        tokens = n1[pl.ds(half * 4, 4)].reshape(512, D)

        def out(t):
            w = qw[t // 2, t % 2].reshape(D, 256)
            return jnp.dot(tokens, w, preferred_element_type=F32)

        def put(ref, n, value):
            ref[n, rows] = value.astype(BF)

        for t, heads in ((0, (0, 3)), (1, (1, 4))):
            o = out(t)
            for j, n in enumerate(heads):
                put(qh, n, o[:, j * 128 : j * 128 + 64] * HEAD ** (-0.5))
                put(kh, n, o[:, j * 128 + 64 : j * 128 + 128])
        o = out(2)
        for j, n in enumerate((0, 1, 3, 4)):
            put(vh, n, o[:, j * 64 : j * 64 + 64])
        o = out(3)
        halves = [
            jnp.concatenate([o[:, j : j + 32], o[:, j + 128 : j + 160]], axis=1)
            for j in (0, 32, 64)
        ]
        put(qh, 2, halves[0] * HEAD ** (-0.5))
        put(kh, 2, halves[1])
        put(vh, 2, halves[2])

    project(zh)
    relay1(-2, 2)
    arrived(tf)
    project(1 - zh)
    arrived(w1r)
    spread1(4)
    arrived(w2r)
    w2r = ring(w2_ref, 2)

    held = w2r
    w2r = [hop(w2_ref, 3, True), hop(w2_ref, 3, False)]
    abase = count[0]
    count[0] += 3

    def give_tile(t, i):
        return pltpu.make_async_remote_copy(
            src_ref=mo.at[i], dst_ref=mx.at[y], send_sem=ss.at[abase + t],
            recv_sem=rs.at[abase + t], device_id={"y": i}, device_id_type=MESH,
        )

    def attend(t, carry):
        i = lax.rem(y + t + 1, 4)
        r = pl.ds(pl.multiple_of(zh * 512 + i * 128, 128), 128)

        @pl.when(t == 2)
        def _():
            arrived(held)
            for d in w2r:
                d.start()

        for n in range(5):
            s = lax.dot_general(qh[n, r], kh[n], NT, preferred_element_type=F32)
            p = jnp.exp(s - jnp.max(s, axis=1, keepdims=True))
            total = jnp.sum(p, axis=1, keepdims=True)
            o = jnp.dot(p.astype(BF), vh[n], preferred_element_type=F32) / total
            mo[i, :, n * 64 : n * 64 + 64] = o.astype(BF)

        @pl.when(t < 3)
        def _():
            give_tile(t, i).start()

        return carry

    lax.fori_loop(0, 4, attend, 0)
    ax = [give_tile(t, lax.rem(y + t + 1, 4)) for t in range(3)]
    sends.extend(ax)

    mx[y] = mo[y]
    arrived(w2r)
    w2r = ring(w2_ref, 4)
    relay1(-3, 3, 4)

    def share(k, lo, hi):
        r = wb.at[c, :, :, lax.rem(x + k, 4), :, lo:hi]
        return start(r, r, sib)

    s1 = [share(k, 0, 640) for k in (0, 1, 3)]
    s2 = [share(k, 640, CUT) for k in (0, 1, 3)]
    arrived(x1b)
    s1.append(share(2, 0, 640))
    s2.append(share(2, 640, CUT))
    arrived(ax)
    arrived(s1)

    cols = []
    for h in range(2):
        acc = None
        for g in range(4):
            w = wb[0, h, g, :, :, 0:640].reshape(320, 640)
            part = jnp.dot(mx[g][:, 0:320], w, preferred_element_type=F32)
            acc = part if acc is None else acc + part
        cols.append(acc)
    resid[...] = (noised[...].astype(F32) + jnp.concatenate(cols, axis=1)).astype(BF)
    n2[y] = normed(resid[...], gain2[...])

    def block(j):
        return n2.at[j]

    gy = spread_y(block)
    arrived(w2r)
    done3 = wb.at[c, :, :, :, :, CUT:1280]
    s2.append(start(done3, done3, sib))
    arrived(s2)

    def feed(blocks, ship):
        m = ROWS * len(blocks)
        tokens = jnp.concatenate([n2[j] for j in blocks], axis=0) if m > ROWS else n2[blocks[0]]
        for h in range(2):

            def hidden(i, carry):
                at = pl.ds(pl.multiple_of(i * 128, 128), 128)
                late = pl.ds(pl.multiple_of(640 + i * 128, 128), 128)
                g = wb[0, h, :, :, :, late].reshape(D, 128)
                v = wb[1, h, :, :, :, at].reshape(D, 128)
                both = jnp.dot(
                    tokens, jnp.concatenate([g, v], axis=1), preferred_element_type=F32
                )
                gate = both[:, 0:128]
                act = 0.5 * gate * (1.0 + lax.erf(gate * 0.5**0.5)) * both[:, 128:256]
                hid[h, 0:m, at] = act.astype(BF)
                return carry

            lax.fori_loop(0, 5, hidden, 0)
        copies = []
        for n in range(5):
            acc = None
            for h in range(2):
                w = wb[1, h, :, :, :, 640:1280].reshape(D, 640)[n * 256 : n * 256 + 256]
                part = lax.dot_general(hid[h, 0:m], w, NT, preferred_element_type=F32)
                acc = part if acc is None else acc + part
            at = pl.ds(n * 256, 256)
            for q, j in enumerate(blocks):
                part = acc[q * ROWS : q * ROWS + ROWS].astype(BF)
                if ship:
                    fs[j, :, at] = part
                    copies.append(start(fs.at[j, :, at], ffin.at[y, :, at], {"y": j}))
                else:
                    ffin[j, :, at] = part
        return copies

    feed([y], False)
    arrived(gy)
    gy = relay_y(block)
    ry = feed([lax.rem(y + 1, 4), lax.rem(y + 3, 4)], True)
    arrived(gy)
    ry += feed([lax.rem(y + 2, 4)], True)
    arrived(ry)
    prediction = resid[...].astype(F32)
    for j in range(4):
        prediction = prediction + ffin[j].astype(F32)
    denoised = (noised[...].astype(F32) - sigma * prediction) / alpha
    den[0] = denoised
    error = denoised - clean[...].astype(F32)
    rowsum = jnp.sum(error * error, axis=1, keepdims=True)
    term = jnp.sum(rowsum, axis=0, keepdims=True) * weight

    def total(buf, slot, group, value):
        buf[slot] = jnp.broadcast_to(value, (8, 128))
        arrived([start(buf.at[slot], buf.at[slot], d) for d in group])
        out = buf[0]
        for j in range(1, len(group) + 1):
            out = out + buf[j]
        return out

    term = total(l1, x * 4 + y, plane, term)
    term = total(l2, z * 2 + c, column, term)
    loss[0, 0] = jnp.max(term)
    assert count[0] <= N_COPIES

    for d in sends:
        d.wait_send()
    for here, away, local in qsend:

        @pl.when(jnp.logical_not(here))
        def _():
            away.wait_send()

    @pl.when(c == 0)
    def _():
        for d in wy:
            d.wait_send()


N_COPIES = 160
CUT = 1024


def shards(
    clean, noise, tsteps, alpha_tab, weight_tab, norm1_gain, norm2_gain,
    wqkv, wout, wgate, wvalue, wdown,
):
    vm = pl.BlockSpec(memory_space=pltpu.VMEM)
    den, loss = pl.pallas_call(
        kernel,
        out_shape=(
            jax.ShapeDtypeStruct((1, ROWS, D), F32),
            jax.ShapeDtypeStruct((1, 1), F32),
        ),
        in_specs=[pl.BlockSpec(memory_space=pltpu.SMEM)] + [vm] * 11,
        out_specs=(vm, pl.BlockSpec(memory_space=pltpu.SMEM)),
        scratch_shapes=[
            pltpu.VMEM((40, 1536), BF),
            pltpu.VMEM((40, 1536), BF),
            pltpu.VMEM((40, 1536), BF),
            pltpu.VMEM((2, 80, 128), BF),
            pltpu.VMEM((4, 80, 256), BF),
            pltpu.VMEM((2, 2, 4, 4, 80, 256), BF),
            pltpu.VMEM((2, 2, 4, 4, 80, 1280), BF),
            pltpu.VMEM((8, ROWS, D), BF),
            pltpu.VMEM((5, L, 64), BF),
            pltpu.VMEM((5, L, 64), BF),
            pltpu.VMEM((5, L, 64), BF),
            pltpu.VMEM((4, ROWS, 384), BF),
            pltpu.VMEM((4, ROWS, 384), BF),
            pltpu.VMEM((4, ROWS, D), BF),
            pltpu.VMEM((2, 256, 640), BF),
            pltpu.VMEM((4, ROWS, D), BF),
            pltpu.VMEM((4, ROWS, D), BF),
            pltpu.VMEM((ROWS, D), BF),
            pltpu.VMEM((ROWS, D), BF),
            pltpu.VMEM((16, 8, 128), F32),
            pltpu.VMEM((16, 8, 128), F32),
            pltpu.SemaphoreType.DMA((N_COPIES,)),
            pltpu.SemaphoreType.DMA((N_COPIES,)),
            pltpu.SemaphoreType.DMA,
        ],
        compiler_params=pltpu.CompilerParams(
            collective_id=0, has_side_effects=True, vmem_limit_bytes=60 * 2**20
        ),
    )(
        tsteps, clean[0], noise[0], alpha_tab[None], weight_tab[None], norm1_gain[None],
        norm2_gain[None], wqkv, wout, wgate, wvalue, wdown.T,
    )
    return den, loss.reshape(())


def solution(mesh):
    split = Mesh(mesh.devices.reshape(4, 4, 2, 2, 4), AXES)
    in_specs = (
        P(DP, MP, None), P(DP, MP, None), P(DP), P(), P(), P(), P(),
        P(None, DP, MP), P(DP, MP), P(DP, MP), P(DP, MP), P(MP, DP),
    )
    out_specs = (P(DP, MP, None), P())
    return jax.shard_map(
        shards, mesh=split, in_specs=in_specs, out_specs=out_specs, check_vma=False
    )
```

```python
import jax
import jax.numpy as jnp
from jax import lax
from jax.experimental import pallas as pl
from jax.experimental.pallas import tpu as pltpu
from jax.sharding import Mesh
from jax.sharding import PartitionSpec as P

D = 1280
HEAD = 64
L = 1024
ROWS = 128
AXES = ("zl", "x", "c", "zh", "y")
DP = ("zl", "x", "c")
MP = ("zh", "y")
MESH = pl.DeviceIdType.MESH
BF = jnp.bfloat16
F32 = jnp.float32
NT = (((1,), (1,)), ((), ()))


def normed(values, gain):
    wide = values.astype(F32)
    center = wide - jnp.mean(wide, axis=-1, keepdims=True)
    spread = jnp.mean(center * center, axis=-1, keepdims=True)
    return (center * lax.rsqrt(spread + 1e-05) * gain).astype(BF)


def kernel(
    tsteps, clean, noise, alpha_tab, weight_tab, gain1, gain2, wqkv, wout, wgate, wvalue, wdown,
    den, loss,
    keep, give, recv, qs, wt, qw, wb, n1, qh, kh, vh, mo, mx, n2, hid, fs, ffin, noised, resid,
    l1, l2, ss, rs, ls,
):
    zl, x, c, zh, y = (lax.axis_index(a) for a in AXES)
    z = zh * 4 + zl
    sends = []
    count = [0]

    def other(name, k, n):
        return {name: lax.rem(lax.axis_index(name) + k, n)}

    def zto(k):
        t = lax.rem(z + k + 8, 8)
        return {"zh": t // 4, "zl": lax.rem(t, 4)}

    def make(src, dst, dev):
        i = count[0]
        count[0] += 1
        d = pltpu.make_async_remote_copy(
            src_ref=src, dst_ref=dst, send_sem=ss.at[i], recv_sem=rs.at[i],
            device_id=dev, device_id_type=MESH,
        )
        sends.append(d)
        return d

    def start(src, dst, dev):
        d = make(src, dst, dev)
        d.start()
        return d

    def arrived(ds):
        for d in ds:
            d.wait_recv()

    ys = [other("y", k, 4) for k in (1, 3, 2)]
    xs = [other("x", k, 4) for k in (1, 3, 2)]
    sib = {"c": 1 - c}
    plane = []
    for k in range(1, 16):
        m = lax.rem(x * 4 + y + k, 16)
        plane.append({"x": m // 4, "y": lax.rem(m, 4)})
    column = []
    for k in range(1, 16):
        m = lax.rem(z * 2 + c + k, 16)
        column.append({"zh": m // 8, "zl": lax.rem(m // 2, 4), "c": lax.rem(m, 2)})
    across = [{"zh": 1 - zh, "y": lax.rem(y + k, 4)} for k in (1, 2, 3)]

    barrier = pltpu.get_barrier_semaphore()
    greet = plane + column + across
    for d in greet:
        pl.semaphore_signal(barrier, 1, device_id=d, device_id_type=MESH)

    step = tsteps[0]
    match = lax.broadcasted_iota(jnp.int32, alpha_tab.shape, 1) == step
    alpha = jnp.sum(jnp.where(match, alpha_tab[...], 0.0), axis=1, keepdims=True)
    weight = jnp.sum(jnp.where(match, weight_tab[...], 0.0), axis=1, keepdims=True) / (L * D)
    sigma = jnp.sqrt(1.0 - alpha * alpha)

    par = lax.rem(y, 2)

    def fold(value, mine_at):
        value = value.astype(BF)
        at = pl.ds(mine_at[1], value.shape[1])

        @pl.when(c == mine_at[0])
        def _():
            keep[:, at] = value

        @pl.when(c != mine_at[0])
        def _():
            give[:, at] = value

    wide = [wqkv[j].astype(F32) for j in range(3)]
    h_a = [jnp.where(par == 0, w[:, 0:64], w[:, 32:96]) for w in wide]
    h_b = [jnp.where(par == 0, w[:, 64:128], w[:, 96:160]) for w in wide]
    h_s = [jnp.where(par == 0, w[:, 128:160], w[:, 0:32]) for w in wide]
    fold(jnp.concatenate([h_a[0], h_a[1]], axis=1), (0, 0))
    fold(jnp.concatenate([h_b[0], h_b[1]], axis=1), (0, 128))
    fold(jnp.concatenate([h_a[2], h_b[2]], axis=1), (1, 0))
    fold(jnp.concatenate(h_s + [jnp.zeros((40, 32), F32)], axis=1), (1, 128))
    fold(jnp.concatenate([wout[...].astype(F32), jnp.zeros((40, 96), F32)], axis=1), (0, 256))
    fold(wvalue[...], (1, 256))
    fold(wgate[...], (0, 896))
    fold(wdown[...], (1, 896))

    noised[...] = (alpha * clean[...].astype(F32) + sigma * noise[...].astype(F32)).astype(BF)
    me = zh * 4 + y
    n1[me] = normed(noised[...], gain1[...].reshape(1, D))

    pl.semaphore_wait(barrier, len(greet))
    s0 = start(give, recv, sib)

    def spread_y(ref):
        return [start(ref(y), ref(y), d) for d in ys[:2]]

    def relay_y(ref):
        low, high = pl.ds(0, 64), pl.ds(64, 64)
        a, b = ref(lax.rem(y + 3, 4)).at[low], ref(lax.rem(y + 1, 4)).at[high]
        return [start(a, a, ys[0]), start(b, b, ys[1])]

    def near(j):
        return n1.at[zh * 4 + j]

    def far(j):
        return n1.at[(1 - zh) * 4 + j]

    arrived([s0])
    mine = keep[...].astype(F32)
    theirs = recv[...].astype(F32)
    first = jnp.where(c == 0, mine, theirs)
    second = jnp.where(c == 0, theirs, mine)
    slab = jnp.concatenate([first, second], axis=0).astype(BF)
    qs[0] = slab[:, 0:128]
    qs[1] = slab[:, 128:256]
    wb[c, zh, zl, x, :, 640:1280] = slab[:, 896:1536]
    ydst = 2 * zh + y // 2
    lane = pl.multiple_of(par * 128, 128)
    qsend = []
    base = count[0]
    count[0] += 2
    for h in range(2):
        here = jnp.logical_and(zh == h, y == ydst)
        dst = qw.at[c, h, zl, x, :, pl.ds(lane, 128)]
        away = pltpu.make_async_remote_copy(
            src_ref=qs.at[h], dst_ref=dst, send_sem=ss.at[base + h], recv_sem=rs.at[base + par],
            device_id={"zh": h, "y": ydst}, device_id_type=MESH,
        )
        local = pltpu.make_async_copy(qs.at[h], dst, ls)
        qsend.append((here, away, local))

        @pl.when(here)
        def _():
            local.start()

        @pl.when(jnp.logical_not(here))
        def _():
            away.start()

    @pl.when(c == 0)
    def _():
        wt[y] = slab[:, 256:512]

    @pl.when(c == 1)
    def _():
        wb[1, zh, zl, x, :, 0:640] = slab[:, 256:896]

    wbase = count[0]
    count[0] += 3
    wy = [
        pltpu.make_async_remote_copy(
            src_ref=wt.at[y], dst_ref=wt.at[y], send_sem=ss.at[wbase + i],
            recv_sem=rs.at[wbase + i], device_id=d, device_id_type=MESH,
        )
        for i, d in enumerate(ys)
    ]

    @pl.when(c == 0)
    def _():
        for d in wy:
            d.start()

    def slab2(k):
        t = lax.rem(z + k + 8, 8)
        return t // 4, lax.rem(t, 4)

    own2 = wb.at[c, zh, zl, x, :, CUT:1280]
    x2 = [start(own2, own2, d) for d in xs]
    ty = spread_y(near)
    tz = []

    def cross(*ks):
        for k in ks:
            r = n1.at[me, pl.ds(32 * k, 32)]
            tz.append(start(r, r, {"zh": 1 - zh}))

    cross(0)

    @pl.when(c == 0)
    def _():
        for d in wy:
            d.wait_recv()
        parts = [wt[j][:, 0:160].astype(F32) for j in range(4)]
        wb[0, zh, zl, x, :, 0:640] = jnp.concatenate(parts, axis=1).astype(BF)

    def hop(ref, k, forward):
        a, b = slab2(-(k - 1) if forward else k - 1)
        r = ref(a, b, None if k < 4 else 1 - int(forward))
        return make(r, r, zto(1 if forward else -1))

    def ring(ref, k):
        ds = [hop(ref, k, True), hop(ref, k, False)]
        for d in ds:
            d.start()
        return ds

    def q_ref(a, b, part):
        rows = slice(None) if part is None else slice(48 * part, 48 + 32 * part)
        return qw.at[c, a, b, x, rows]

    def wa_ref(a, b, part):
        cols = slice(0, 640) if part is None else slice(384 * part, 384 + 256 * part)
        return wb.at[c, a, b, x, :, cols]

    def wc_ref(a, b, part):
        cols = slice(640, CUT) if part is None else slice(640 + 128 * part, 768 + 128 * part)
        return wb.at[c, a, b, x, :, cols]

    def w2_ref(a, b, part):
        which = slice(None) if part is None else slice(2 * part, 2 * part + 2)
        return wb.at[c, a, b, which, :, CUT:1280]

    def spreader(ref):
        got = {}

        def spread(*ks):
            for k in ks:
                r = ref(*slab2(k), None)
                got[k] = [start(r, r, d) for d in xs[:2]]

        return got, spread

    def relayer(got, lo, hi):
        sent = []

        def relay(*ks):
            for k in ks:
                arrived(got[k])
                a, b = slab2(k)
                turn = 1 + 2 * a
                r = wb.at[c, a, b, lax.rem(x + 4 - turn, 4), :, lo:hi]
                sent.append(start(r, r, {"x": lax.rem(x + turn, 4)}))

        return sent, relay

    xa, spreada = spreader(wa_ref)
    xc, spreadc = spreader(wc_ref)
    xa2, relaya = relayer(xa, 0, 640)
    xc2, relayc = relayer(xc, 640, CUT)

    ar = ring(wa_ref, 1)
    spreada(0)

    homes = (jnp.logical_and(zh == 0, y == 0), jnp.logical_and(zh == 1, y == 3))
    alone = jnp.logical_or(*homes)
    for p in range(2):
        landed = pltpu.make_async_remote_copy(
            src_ref=qs.at[0], dst_ref=qw.at[c, zh, zl, x, :, pl.ds(p * 128, 128)],
            send_sem=ss.at[base], recv_sem=rs.at[base + p], device_id=sib, device_id_type=MESH,
        )
        self_slot = jnp.logical_and(alone, par == p)

        @pl.when(jnp.logical_not(self_slot))
        def _():
            landed.wait_recv()

    for here, away, local in qsend:

        @pl.when(here)
        def _():
            local.wait()

    xq = []

    def spreadq(*ks):
        for k in ks:
            r = q_ref(*slab2(k), None)
            xq.extend([start(r, r, d) for d in xs[:2]])

    def shareq(k):
        r = qw.at[c, :, :, lax.rem(x + k, 4)]
        return make(r, r, sib)

    def share(k, lo, hi):
        r = wb.at[c, :, :, lax.rem(x + k, 4), :, lo:hi]
        return make(r, r, sib)

    s2 = []

    def share2(*ks):
        for k in ks:
            r = w2_ref(*slab2(k), None)
            s2.append(start(r, r, sib))

    def spread_far(low):
        r = far(y).at[pl.ds(low, 64)]
        return [start(r, r, d) for d in ys[:2]]

    er = ring(q_ref, 1)
    spreadq(0)
    cross(1)
    arrived(er)
    er = ring(q_ref, 2)
    spreadq(-1, 1)
    cross(2)
    arrived(ar)
    ar = ring(wa_ref, 2)
    spreada(-1, 1)
    arrived(ty)
    ty = relay_y(near)
    arrived(er)
    er = ring(q_ref, 3)
    spreadq(-2, 2)
    cross(3)
    arrived(tz[0:2])
    tf = spread_far(0)
    arrived(er)
    er = ring(q_ref, 4)
    spreadq(-3, 3)
    arrived(ar)
    ar = ring(wa_ref, 3)
    arrived(er)
    spreadq(4)
    spreada(-2, 2)
    arrived(tz[2:4])
    tg = spread_far(64)
    arrived(tf)
    r = far(lax.rem(y + 3, 4)).at[pl.ds(0, 64)]
    tr = [start(r, r, ys[0])]
    arrived(x2)
    w2r = ring(w2_ref, 1)
    share2(0)
    arrived(xq)
    rq = []
    for a in range(2):
        turn = 1 + 2 * a
        r = qw.at[c, a, :, lax.rem(x + 4 - turn, 4)]
        rq.append(start(r, r, {"x": lax.rem(x + turn, 4)}))
    sq = [shareq(k) for k in (0, 1, 3)]
    for d in sq:
        d.start()
    relaya(0)
    arrived(ar)
    ar = ring(wa_ref, 4)
    spreada(-3, 3)
    relaya(-1, 1)
    arrived(tg)
    r = far(lax.rem(y + 1, 4)).at[pl.ds(64, 64)]
    tr.append(start(r, r, ys[1]))
    cr = ring(wc_ref, 1)
    arrived(rq)
    sq.append(shareq(2))
    sq[3].start()
    arrived(w2r)
    w2r = ring(w2_ref, 2)
    share2(-1, 1)
    arrived(ty)
    arrived(sq)

    def project(half):
        rows = pl.ds(pl.multiple_of(half * 512, 512), 512)
        tokens = n1[pl.ds(half * 4, 4)].reshape(512, D)

        def out(t):
            w = qw[t // 2, t % 2].reshape(D, 256)
            return jnp.dot(tokens, w, preferred_element_type=F32)

        def put(ref, n, value):
            ref[n, rows] = value.astype(BF)

        for t, heads in ((0, (0, 3)), (1, (1, 4))):
            o = out(t)
            for j, n in enumerate(heads):
                put(qh, n, o[:, j * 128 : j * 128 + 64] * HEAD ** (-0.5))
                put(kh, n, o[:, j * 128 + 64 : j * 128 + 128])
        o = out(2)
        for j, n in enumerate((0, 1, 3, 4)):
            put(vh, n, o[:, j * 64 : j * 64 + 64])
        o = out(3)
        halves = [
            jnp.concatenate([o[:, j : j + 32], o[:, j + 128 : j + 160]], axis=1)
            for j in (0, 32, 64)
        ]
        put(qh, 2, halves[0] * HEAD ** (-0.5))
        put(kh, 2, halves[1])
        put(vh, 2, halves[2])

    project(zh)
    arrived(ar)
    spreada(4)
    relaya(-2, 2)
    arrived(cr)
    cr = ring(wc_ref, 2)
    spreadc(0)
    arrived(tr)
    project(1 - zh)

    ax = []

    def attend(k):
        i = lax.rem(y + k, 4)
        r = pl.ds(pl.multiple_of(zh * 512 + i * 128, 128), 128)
        for n in range(5):
            s = lax.dot_general(qh[n, r], kh[n], NT, preferred_element_type=F32)
            p = jnp.exp(s - jnp.max(s, axis=1, keepdims=True))
            total = jnp.sum(p, axis=1, keepdims=True)
            o = jnp.dot(p.astype(BF), vh[n], preferred_element_type=F32) / total
            mo[i, :, n * 64 : n * 64 + 64] = o.astype(BF)
        if k:
            ax.append(start(mo.at[i], mx.at[y], {"y": i}))

    attend(2)
    relaya(-3, 3)
    spreadc(-1, 1)
    arrived(w2r)
    w2r = ring(w2_ref, 3)
    share2(-2, 2)
    attend(1)
    arrived(cr)
    cr = ring(wc_ref, 3)
    relaya(4)
    spreadc(-2, 2)
    s1 = [share(k, 0, 640) for k in (0, 1, 3)]
    for d in s1:
        d.start()
    attend(3)
    arrived(w2r)
    w2r = ring(w2_ref, 4)
    share2(-3, 3)
    relayc(0, -1, 1)
    attend(0)
    mx[y] = mo[y]
    arrived(cr)
    cr = ring(wc_ref, 4)
    spreadc(-3, 3)
    arrived(xa2)
    s1.append(share(2, 0, 640))
    s1[3].start()
    relayc(-2, 2)
    arrived(ax)
    arrived(s1)

    cols = []
    for h in range(2):
        acc = None
        for g in range(4):
            w = wb[0, h, g, :, :, 0:640].reshape(320, 640)
            part = jnp.dot(mx[g][:, 0:320], w, preferred_element_type=F32)
            acc = part if acc is None else acc + part
        cols.append(acc)
    resid[...] = (noised[...].astype(F32) + jnp.concatenate(cols, axis=1)).astype(BF)
    n2[y] = normed(resid[...], gain2[...].reshape(1, D))

    gy = [start(n2.at[y], n2.at[y], d) for d in ys[:2]]
    arrived(cr)
    spreadc(4)
    relayc(-3, 3)
    arrived(w2r)
    share2(4)
    relayc(4)
    s1b = [share(k, 640, CUT) for k in (0, 1, 3)]
    for d in s1b:
        d.start()
    arrived(gy)
    up, down = lax.rem(y + 1, 4), lax.rem(y + 3, 4)
    gr = []
    for j, low, d in ((down, 0, ys[0]), (up, 64, ys[1])):
        r = n2.at[j, pl.ds(low, 64)]
        gr.append(start(r, r, d))
    arrived(xc2)
    s1b.append(share(2, 640, CUT))
    s1b[3].start()
    arrived(s2)
    arrived(s1b)

    def feed(blocks, ship):
        m = sum(n for j, r, n in blocks)
        tokens = jnp.concatenate([n2[j, r : r + n] for j, r, n in blocks], axis=0)
        for h in range(2):

            def hidden(i, carry):
                at = pl.ds(pl.multiple_of(i * 128, 128), 128)
                late = pl.ds(pl.multiple_of(640 + i * 128, 128), 128)
                g = wb[0, h, :, :, :, late].reshape(D, 128)
                v = wb[1, h, :, :, :, at].reshape(D, 128)
                both = jnp.dot(
                    tokens, jnp.concatenate([g, v], axis=1), preferred_element_type=F32
                )
                gate = both[:, 0:128]
                act = 0.5 * gate * (1.0 + lax.erf(gate * 0.5**0.5)) * both[:, 128:256]
                hid[h, 0:m, at] = act.astype(BF)
                return carry

            lax.fori_loop(0, 5, hidden, 0)
        copies = []
        for n in range(5):
            acc = None
            for h in range(2):
                w = wb[1, h, :, :, :, 640:1280].reshape(D, 640)[n * 256 : n * 256 + 256]
                part = lax.dot_general(hid[h, 0:m], w, NT, preferred_element_type=F32)
                acc = part if acc is None else acc + part
            at = pl.ds(n * 256, 256)
            q = 0
            for j, r, k in blocks:
                part = acc[q : q + k].astype(BF)
                q += k
                rows = pl.ds(r, k)
                if ship:
                    fs[j, rows, at] = part
                    copies.append(start(fs.at[j, rows, at], ffin.at[y, rows, at], {"y": j}))
                else:
                    ffin[j, rows, at] = part
        return copies

    ry = feed([(up, 0, ROWS), (down, 0, ROWS)], True)
    arrived(gr)
    ry += feed([(lax.rem(y + 2, 4), 0, ROWS)], True)
    feed([(y, 0, ROWS)], False)
    arrived(ry)
    prediction = resid[...].astype(F32)
    for j in range(4):
        prediction = prediction + ffin[j].astype(F32)
    denoised = (noised[...].astype(F32) - sigma * prediction) / alpha
    den[0] = denoised
    error = denoised - clean[...].astype(F32)
    rowsum = jnp.sum(error * error, axis=1, keepdims=True)
    term = jnp.sum(rowsum, axis=0, keepdims=True) * weight

    def total(buf, slot, group, value):
        buf[slot] = jnp.broadcast_to(value, (8, 128))
        arrived([start(buf.at[slot], buf.at[slot], d) for d in group])
        out = buf[0]
        for j in range(1, len(group) + 1):
            out = out + buf[j]
        return out

    term = total(l1, x * 4 + y, plane, term)
    term = total(l2, z * 2 + c, column, term)
    loss[0, 0] = jnp.max(term)
    assert count[0] <= N_COPIES

    for d in sends:
        d.wait_send()
    for here, away, local in qsend:

        @pl.when(jnp.logical_not(here))
        def _():
            away.wait_send()

    @pl.when(c == 0)
    def _():
        for d in wy:
            d.wait_send()


N_COPIES = 208
CUT = 896


def shards(
    clean, noise, tsteps, alpha_tab, weight_tab, norm1_gain, norm2_gain,
    wqkv, wout, wgate, wvalue, wdown,
):
    vm = pl.BlockSpec(memory_space=pltpu.VMEM)
    den, loss = pl.pallas_call(
        kernel,
        out_shape=(
            jax.ShapeDtypeStruct((1, ROWS, D), F32),
            jax.ShapeDtypeStruct((1, 1), F32),
        ),
        in_specs=[pl.BlockSpec(memory_space=pltpu.SMEM)] + [vm] * 11,
        out_specs=(vm, pl.BlockSpec(memory_space=pltpu.SMEM)),
        scratch_shapes=[
            pltpu.VMEM((40, 1536), BF),
            pltpu.VMEM((40, 1536), BF),
            pltpu.VMEM((40, 1536), BF),
            pltpu.VMEM((2, 80, 128), BF),
            pltpu.VMEM((4, 80, 256), BF),
            pltpu.VMEM((2, 2, 4, 4, 80, 256), BF),
            pltpu.VMEM((2, 2, 4, 4, 80, 1280), BF),
            pltpu.VMEM((8, ROWS, D), BF),
            pltpu.VMEM((5, L, 64), BF),
            pltpu.VMEM((5, L, 64), BF),
            pltpu.VMEM((5, L, 64), BF),
            pltpu.VMEM((4, ROWS, 384), BF),
            pltpu.VMEM((4, ROWS, 384), BF),
            pltpu.VMEM((4, ROWS, D), BF),
            pltpu.VMEM((2, 256, 640), BF),
            pltpu.VMEM((4, ROWS, D), BF),
            pltpu.VMEM((4, ROWS, D), BF),
            pltpu.VMEM((ROWS, D), BF),
            pltpu.VMEM((ROWS, D), BF),
            pltpu.VMEM((16, 8, 128), F32),
            pltpu.VMEM((16, 8, 128), F32),
            pltpu.SemaphoreType.DMA((N_COPIES,)),
            pltpu.SemaphoreType.DMA((N_COPIES,)),
            pltpu.SemaphoreType.DMA,
        ],
        compiler_params=pltpu.CompilerParams(
            collective_id=0, has_side_effects=True, vmem_limit_bytes=60 * 2**20
        ),
    )(
        tsteps, clean[0], noise[0], alpha_tab[None], weight_tab[None], norm1_gain,
        norm2_gain, wqkv, wout, wgate, wvalue, wdown.T,
    )
    return den, loss.reshape(())


def solution(mesh):
    split = Mesh(mesh.devices.reshape(4, 4, 2, 2, 4), AXES)
    in_specs = (
        P(DP, MP, None), P(DP, MP, None), P(DP), P(), P(), P(), P(),
        P(None, DP, MP), P(DP, MP), P(DP, MP), P(DP, MP), P(MP, DP),
    )
    out_specs = (P(DP, MP, None), P())
    return jax.shard_map(
        shards, mesh=split, in_specs=in_specs, out_specs=out_specs, check_vma=False
    )
```

```python
import jax
import jax.numpy as jnp
from jax import lax
from jax.experimental import pallas as pl
from jax.experimental.pallas import tpu as pltpu
from jax.sharding import Mesh
from jax.sharding import PartitionSpec as P

D = 1280
HEAD = 64
L = 1024
ROWS = 128
AXES = ("zl", "x", "c", "zh", "y")
DP = ("zl", "x", "c")
MP = ("zh", "y")
MESH = pl.DeviceIdType.MESH
BF = jnp.bfloat16
F32 = jnp.float32
NT = (((1,), (1,)), ((), ()))


def normed(values, gain):
    wide = values.astype(F32)
    center = wide - jnp.mean(wide, axis=-1, keepdims=True)
    spread = jnp.mean(center * center, axis=-1, keepdims=True)
    return (center * lax.rsqrt(spread + 1e-05) * gain).astype(BF)


def kernel(
    tsteps, clean, noise, alpha_tab, weight_tab, gain1, gain2, wqkv, wout, wgate, wvalue, wdown,
    den, loss,
    keep, give, recv, qs, wt, qw, wb, n1, qh, kh, vh, mo, mx, n2, hid, fs, ffin, noised, resid,
    l1, l2, ss, rs, ls,
):
    zl, x, c, zh, y = (lax.axis_index(a) for a in AXES)
    z = zh * 4 + zl
    sends = []
    count = [0]

    def other(name, k, n):
        return {name: lax.rem(lax.axis_index(name) + k, n)}

    def zto(k):
        t = lax.rem(z + k + 8, 8)
        return {"zh": t // 4, "zl": lax.rem(t, 4)}

    def make(src, dst, dev):
        i = count[0]
        count[0] += 1
        d = pltpu.make_async_remote_copy(
            src_ref=src, dst_ref=dst, send_sem=ss.at[i], recv_sem=rs.at[i],
            device_id=dev, device_id_type=MESH,
        )
        sends.append(d)
        return d

    def start(src, dst, dev):
        d = make(src, dst, dev)
        d.start()
        return d

    def arrived(ds):
        for d in ds:
            d.wait_recv()

    ys = [other("y", k, 4) for k in (1, 3, 2)]
    xs = [other("x", k, 4) for k in (1, 3, 2)]
    sib = {"c": 1 - c}
    plane = []
    for k in range(1, 16):
        m = lax.rem(x * 4 + y + k, 16)
        plane.append({"x": m // 4, "y": lax.rem(m, 4)})
    column = []
    for k in range(1, 16):
        m = lax.rem(z * 2 + c + k, 16)
        column.append({"zh": m // 8, "zl": lax.rem(m // 2, 4), "c": lax.rem(m, 2)})
    across = [{"zh": 1 - zh, "y": lax.rem(y + k, 4)} for k in (1, 2, 3)]

    barrier = pltpu.get_barrier_semaphore()
    greet = plane + column + across
    for d in greet:
        pl.semaphore_signal(barrier, 1, device_id=d, device_id_type=MESH)

    step = tsteps[0]
    match = lax.broadcasted_iota(jnp.int32, alpha_tab.shape, 1) == step
    alpha = jnp.sum(jnp.where(match, alpha_tab[...], 0.0), axis=1, keepdims=True)
    weight = jnp.sum(jnp.where(match, weight_tab[...], 0.0), axis=1, keepdims=True) / (L * D)
    sigma = jnp.sqrt(1.0 - alpha * alpha)

    par = lax.rem(y, 2)

    def fold(value, mine_at):
        value = value.astype(BF)
        at = pl.ds(mine_at[1], value.shape[1])

        @pl.when(c == mine_at[0])
        def _():
            keep[:, at] = value

        @pl.when(c != mine_at[0])
        def _():
            give[:, at] = value

    wide = [wqkv[j].astype(F32) for j in range(3)]
    h_a = [jnp.where(par == 0, w[:, 0:64], w[:, 32:96]) for w in wide]
    h_b = [jnp.where(par == 0, w[:, 64:128], w[:, 96:160]) for w in wide]
    h_s = [jnp.where(par == 0, w[:, 128:160], w[:, 0:32]) for w in wide]
    fold(jnp.concatenate([h_a[0], h_a[1]], axis=1), (0, 0))
    fold(jnp.concatenate([h_b[0], h_b[1]], axis=1), (0, 128))
    fold(jnp.concatenate([h_a[2], h_b[2]], axis=1), (1, 0))
    fold(jnp.concatenate(h_s + [jnp.zeros((40, 32), F32)], axis=1), (1, 128))
    fold(jnp.concatenate([wout[...].astype(F32), jnp.zeros((40, 96), F32)], axis=1), (0, 256))
    fold(wvalue[...], (1, 256))
    fold(wgate[...], (0, 896))
    fold(wdown[...], (1, 896))

    noised[...] = (alpha * clean[...].astype(F32) + sigma * noise[...].astype(F32)).astype(BF)
    me = zh * 4 + y
    n1[me] = normed(noised[...], gain1[...].reshape(1, D))

    pl.semaphore_wait(barrier, len(greet))
    s0 = start(give, recv, sib)
    tz = []

    def cross(*ks):
        for k in ks:
            r = n1.at[me, pl.ds(32 * k, 32)]
            tz.append(start(r, r, {"zh": 1 - zh}))

    cross(0)

    def spread_y(ref):
        return [start(ref(y), ref(y), d) for d in ys[:2]]

    def relay_y(ref):
        low, high = pl.ds(0, 64), pl.ds(64, 64)
        a, b = ref(lax.rem(y + 3, 4)).at[low], ref(lax.rem(y + 1, 4)).at[high]
        return [start(a, a, ys[0]), start(b, b, ys[1])]

    def near(j):
        return n1.at[zh * 4 + j]

    def far(j):
        return n1.at[(1 - zh) * 4 + j]

    arrived([s0])
    mine = keep[...].astype(F32)
    theirs = recv[...].astype(F32)
    first = jnp.where(c == 0, mine, theirs)
    second = jnp.where(c == 0, theirs, mine)
    slab = jnp.concatenate([first, second], axis=0).astype(BF)
    qs[0] = slab[:, 0:128]
    qs[1] = slab[:, 128:256]
    wb[c, zh, zl, x, :, 640:1280] = slab[:, 896:1536]
    ydst = 2 * zh + y // 2
    lane = pl.multiple_of(par * 128, 128)
    qsend = []
    base = count[0]
    count[0] += 2
    for h in range(2):
        here = jnp.logical_and(zh == h, y == ydst)
        dst = qw.at[c, h, zl, x, :, pl.ds(lane, 128)]
        away = pltpu.make_async_remote_copy(
            src_ref=qs.at[h], dst_ref=dst, send_sem=ss.at[base + h], recv_sem=rs.at[base + par],
            device_id={"zh": h, "y": ydst}, device_id_type=MESH,
        )
        local = pltpu.make_async_copy(qs.at[h], dst, ls)
        qsend.append((here, away, local))

        @pl.when(here)
        def _():
            local.start()

        @pl.when(jnp.logical_not(here))
        def _():
            away.start()

    @pl.when(c == 0)
    def _():
        wt[y] = slab[:, 256:512]

    @pl.when(c == 1)
    def _():
        wb[1, zh, zl, x, :, 0:640] = slab[:, 256:896]

    wbase = count[0]
    count[0] += 3
    wy = [
        pltpu.make_async_remote_copy(
            src_ref=wt.at[y], dst_ref=wt.at[y], send_sem=ss.at[wbase + i],
            recv_sem=rs.at[wbase + i], device_id=d, device_id_type=MESH,
        )
        for i, d in enumerate(ys)
    ]

    @pl.when(c == 0)
    def _():
        for d in wy:
            d.start()

    def slab2(k):
        t = lax.rem(z + k + 8, 8)
        return t // 4, lax.rem(t, 4)

    def hop(ref, k, forward):
        a, b = slab2(-(k - 1) if forward else k - 1)
        r = ref(a, b, None if k < 4 else 1 - int(forward))
        return make(r, r, zto(1 if forward else -1))

    def ring(ref, k):
        ds = [hop(ref, k, True), hop(ref, k, False)]
        for d in ds:
            d.start()
        return ds

    def q_ref(a, b, part):
        rows = slice(None) if part is None else slice(48 * part, 48 + 32 * part)
        return qw.at[c, a, b, x, rows]

    def wa_ref(a, b, part):
        cols = slice(0, 640) if part is None else slice(384 * part, 384 + 256 * part)
        return wb.at[c, a, b, x, :, cols]

    def wc_ref(a, b, part):
        cols = slice(640, CUT) if part is None else slice(640 + 128 * part, 768 + 128 * part)
        return wb.at[c, a, b, x, :, cols]

    def w2_ref(a, b, part):
        which = slice(None) if part is None else slice(2 * part, 2 * part + 2)
        return wb.at[c, a, b, which, :, CUT:1280]

    def spreader(ref):
        got = {}

        def spread(*ks):
            for k in ks:
                r = ref(*slab2(k), None)
                got[k] = [start(r, r, d) for d in xs[:2]]

        return got, spread

    def relayer(got, lo, hi):
        sent = []

        def relay(*ks):
            for k in ks:
                arrived(got[k])
                a, b = slab2(k)
                turn = 1 + 2 * a
                r = wb.at[c, a, b, lax.rem(x + 4 - turn, 4), :, lo:hi]
                sent.append(start(r, r, {"x": lax.rem(x + turn, 4)}))

        return sent, relay

    xa, spreada = spreader(wa_ref)
    xc, spreadc = spreader(wc_ref)
    xa2, relaya = relayer(xa, 0, 640)
    xc2, relayc = relayer(xc, 640, CUT)

    own2 = wb.at[c, zh, zl, x, :, CUT:1280]
    x2 = [start(own2, own2, d) for d in xs]
    cr = ring(wc_ref, 1)
    spreadc(0)
    ty = spread_y(near)
    @pl.when(c == 0)
    def _():
        for d in wy:
            d.wait_recv()
        parts = [wt[j][:, 0:160].astype(F32) for j in range(4)]
        wb[0, zh, zl, x, :, 0:640] = jnp.concatenate(parts, axis=1).astype(BF)

    ar = ring(wa_ref, 1)
    spreada(0)

    homes = (jnp.logical_and(zh == 0, y == 0), jnp.logical_and(zh == 1, y == 3))
    alone = jnp.logical_or(*homes)
    for p in range(2):
        landed = pltpu.make_async_remote_copy(
            src_ref=qs.at[0], dst_ref=qw.at[c, zh, zl, x, :, pl.ds(p * 128, 128)],
            send_sem=ss.at[base], recv_sem=rs.at[base + p], device_id=sib, device_id_type=MESH,
        )
        self_slot = jnp.logical_and(alone, par == p)

        @pl.when(jnp.logical_not(self_slot))
        def _():
            landed.wait_recv()

    for here, away, local in qsend:

        @pl.when(here)
        def _():
            local.wait()

    xq, spreadq = spreader(q_ref)
    rq = []

    def relayq(*ks):
        for k in ks:
            arrived(xq[k])
            a, b = slab2(k)
            turn = 1 + 2 * a
            r = qw.at[c, a, b, lax.rem(x + 4 - turn, 4)]
            rq.append(start(r, r, {"x": lax.rem(x + turn, 4)}))

    def shareq(k):
        r = qw.at[c, :, :, lax.rem(x + k, 4)]
        return make(r, r, sib)

    def share(k, lo, hi):
        r = wb.at[c, :, :, lax.rem(x + k, 4), :, lo:hi]
        return make(r, r, sib)

    s2 = []

    def share2(*ks):
        for k in ks:
            r = w2_ref(*slab2(k), None)
            s2.append(start(r, r, sib))

    def spread_far(low):
        r = far(y).at[pl.ds(low, 64)]
        return [start(r, r, d) for d in ys[:2]]

    er = ring(q_ref, 1)
    spreadq(0)
    cross(1)
    arrived(er)
    er = ring(q_ref, 2)
    spreadq(-1, 1)
    cross(2)
    arrived(ar)
    ar = ring(wa_ref, 2)
    spreada(-1, 1)
    arrived(ty)
    ty = relay_y(near)
    arrived(er)
    er = ring(q_ref, 3)
    spreadq(-2, 2)
    relayq(0)
    cross(3)
    arrived(tz[0:2])
    tf = spread_far(0)
    arrived(ar)
    ar = ring(wa_ref, 3)
    spreada(-2, 2)
    arrived(er)
    er = ring(q_ref, 4)
    spreadq(-3, 3)
    relayq(-1, 1)
    arrived(er)
    spreadq(4)
    relayq(-2, 2)
    arrived(tz[2:4])
    tg = spread_far(64)
    arrived(ar)
    ar = ring(wa_ref, 4)
    arrived(tf)
    r = far(lax.rem(y + 3, 4)).at[pl.ds(0, 64)]
    tr = [start(r, r, ys[0])]
    arrived(x2)
    w2r = ring(w2_ref, 1)
    share2(0)
    relayq(-3, 3, 4)
    sq = [shareq(k) for k in (0, 1, 3)]
    for d in sq:
        d.start()
    spreada(-3, 3)
    relaya(0, -1, 1)
    arrived(tg)
    r = far(lax.rem(y + 1, 4)).at[pl.ds(64, 64)]
    tr.append(start(r, r, ys[1]))
    arrived(rq)
    sq.append(shareq(2))
    sq[3].start()
    arrived(ar)
    spreada(4)
    arrived(cr)
    cr = ring(wc_ref, 2)
    arrived(w2r)
    w2r = ring(w2_ref, 2)
    share2(-1, 1)
    arrived(ty)
    arrived(sq)

    def project(half):
        rows = pl.ds(pl.multiple_of(half * 512, 512), 512)
        tokens = n1[pl.ds(half * 4, 4)].reshape(512, D)

        def out(t):
            w = qw[t // 2, t % 2].reshape(D, 256)
            return jnp.dot(tokens, w, preferred_element_type=F32)

        def put(ref, n, value):
            ref[n, rows] = value.astype(BF)

        for t, heads in ((0, (0, 3)), (1, (1, 4))):
            o = out(t)
            for j, n in enumerate(heads):
                put(qh, n, o[:, j * 128 : j * 128 + 64] * HEAD ** (-0.5))
                put(kh, n, o[:, j * 128 + 64 : j * 128 + 128])
        o = out(2)
        for j, n in enumerate((0, 1, 3, 4)):
            put(vh, n, o[:, j * 64 : j * 64 + 64])
        o = out(3)
        halves = [
            jnp.concatenate([o[:, j : j + 32], o[:, j + 128 : j + 160]], axis=1)
            for j in (0, 32, 64)
        ]
        put(qh, 2, halves[0] * HEAD ** (-0.5))
        put(kh, 2, halves[1])
        put(vh, 2, halves[2])

    project(zh)
    relaya(-2, 2)
    spreadc(-1, 1)
    arrived(tr)
    project(1 - zh)

    ax = []

    def attend(k):
        i = lax.rem(y + k, 4)
        r = pl.ds(pl.multiple_of(zh * 512 + i * 128, 128), 128)
        for n in range(5):
            s = lax.dot_general(qh[n, r], kh[n], NT, preferred_element_type=F32)
            p = jnp.exp(s - jnp.max(s, axis=1, keepdims=True))
            total = jnp.sum(p, axis=1, keepdims=True)
            o = jnp.dot(p.astype(BF), vh[n], preferred_element_type=F32) / total
            mo[i, :, n * 64 : n * 64 + 64] = o.astype(BF)
        if k:
            ax.append(start(mo.at[i], mx.at[y], {"y": i}))

    attend(2)
    relaya(-3, 3)
    arrived(w2r)
    w2r = ring(w2_ref, 3)
    share2(-2, 2)
    attend(1)
    arrived(cr)
    cr = ring(wc_ref, 3)
    relaya(4)
    spreadc(-2, 2)
    s1 = [share(k, 0, 640) for k in (0, 1, 3)]
    for d in s1:
        d.start()
    attend(3)
    relayc(0, -1, 1)
    attend(0)
    mx[y] = mo[y]
    arrived(w2r)
    w2r = ring(w2_ref, 4)
    share2(-3, 3)
    arrived(cr)
    cr = ring(wc_ref, 4)
    spreadc(-3, 3)
    arrived(xa2)
    s1.append(share(2, 0, 640))
    s1[3].start()
    relayc(-2, 2)
    arrived(ax)
    arrived(s1)

    cols = []
    for h in range(2):
        acc = None
        for g in range(4):
            w = wb[0, h, g, :, :, 0:640].reshape(320, 640)
            part = jnp.dot(mx[g][:, 0:320], w, preferred_element_type=F32)
            acc = part if acc is None else acc + part
        cols.append(acc)
    resid[...] = (noised[...].astype(F32) + jnp.concatenate(cols, axis=1)).astype(BF)
    n2[y] = normed(resid[...], gain2[...].reshape(1, D))

    gy = [start(n2.at[y], n2.at[y], d) for d in ys[:2]]
    arrived(cr)
    spreadc(4)
    relayc(-3, 3)
    arrived(w2r)
    share2(4)
    relayc(4)
    s1b = [share(k, 640, CUT) for k in (0, 1, 3)]
    for d in s1b:
        d.start()
    arrived(xc2)
    s1b.append(share(2, 640, CUT))
    s1b[3].start()
    arrived(s2)
    arrived(s1b)

    def feed(blocks, ship):
        m = sum(n for j, r, n in blocks)
        tokens = jnp.concatenate([n2[j, r : r + n] for j, r, n in blocks], axis=0)
        for h in range(2):

            def hidden(i, carry):
                at = pl.ds(pl.multiple_of(i * 128, 128), 128)
                late = pl.ds(pl.multiple_of(640 + i * 128, 128), 128)
                g = wb[0, h, :, :, :, late].reshape(D, 128)
                v = wb[1, h, :, :, :, at].reshape(D, 128)
                both = jnp.dot(
                    tokens, jnp.concatenate([g, v], axis=1), preferred_element_type=F32
                )
                gate = both[:, 0:128]
                act = 0.5 * gate * (1.0 + lax.erf(gate * 0.5**0.5)) * both[:, 128:256]
                hid[h, 0:m, at] = act.astype(BF)
                return carry

            lax.fori_loop(0, 5, hidden, 0, unroll=True)
        copies = []
        for n in range(5):
            acc = None
            for h in range(2):
                w = wb[1, h, :, :, :, 640:1280].reshape(D, 640)[n * 256 : n * 256 + 256]
                part = lax.dot_general(hid[h, 0:m], w, NT, preferred_element_type=F32)
                acc = part if acc is None else acc + part
            at = pl.ds(n * 256, 256)
            q = 0
            for j, r, k in blocks:
                part = acc[q : q + k].astype(BF)
                q += k
                rows = pl.ds(r, k)
                if ship:
                    fs[j, rows, at] = part
                    copies.append(start(fs.at[j, rows, at], ffin.at[y, rows, at], {"y": j}))
                else:
                    ffin[j, rows, at] = part
        return copies

    feed([(y, 0, ROWS)], False)
    arrived(gy)
    up, down = lax.rem(y + 1, 4), lax.rem(y + 3, 4)
    gr = []
    for j, low, d in ((down, 0, ys[0]), (up, 64, ys[1])):
        r = n2.at[j, pl.ds(low, 64)]
        gr.append(start(r, r, d))
    ry = feed([(up, 0, ROWS), (down, 0, ROWS)], True)
    arrived(gr)
    ry += feed([(lax.rem(y + 2, 4), 0, ROWS)], True)
    arrived(ry)
    prediction = resid[...].astype(F32)
    for j in range(4):
        prediction = prediction + ffin[j].astype(F32)
    denoised = (noised[...].astype(F32) - sigma * prediction) / alpha
    den[0] = denoised
    error = denoised - clean[...].astype(F32)
    rowsum = jnp.sum(error * error, axis=1, keepdims=True)
    term = jnp.sum(rowsum, axis=0, keepdims=True) * weight

    def total(buf, slot, group, value):
        buf[slot] = jnp.broadcast_to(value, (8, 128))
        arrived([start(buf.at[slot], buf.at[slot], d) for d in group])
        out = buf[0]
        for j in range(1, len(group) + 1):
            out = out + buf[j]
        return out

    term = total(l1, x * 4 + y, plane, term)
    term = total(l2, z * 2 + c, column, term)
    loss[0, 0] = jnp.max(term)
    assert count[0] <= N_COPIES

    for d in sends:
        d.wait_send()
    for here, away, local in qsend:

        @pl.when(jnp.logical_not(here))
        def _():
            away.wait_send()

    @pl.when(c == 0)
    def _():
        for d in wy:
            d.wait_send()


N_COPIES = 224
CUT = 896


def shards(
    clean, noise, tsteps, alpha_tab, weight_tab, norm1_gain, norm2_gain,
    wqkv, wout, wgate, wvalue, wdown,
):
    vm = pl.BlockSpec(memory_space=pltpu.VMEM)
    den, loss = pl.pallas_call(
        kernel,
        out_shape=(
            jax.ShapeDtypeStruct((1, ROWS, D), F32),
            jax.ShapeDtypeStruct((1, 1), F32),
        ),
        in_specs=[pl.BlockSpec(memory_space=pltpu.SMEM)] + [vm] * 11,
        out_specs=(vm, pl.BlockSpec(memory_space=pltpu.SMEM)),
        scratch_shapes=[
            pltpu.VMEM((40, 1536), BF),
            pltpu.VMEM((40, 1536), BF),
            pltpu.VMEM((40, 1536), BF),
            pltpu.VMEM((2, 80, 128), BF),
            pltpu.VMEM((4, 80, 256), BF),
            pltpu.VMEM((2, 2, 4, 4, 80, 256), BF),
            pltpu.VMEM((2, 2, 4, 4, 80, 1280), BF),
            pltpu.VMEM((8, ROWS, D), BF),
            pltpu.VMEM((5, L, 64), BF),
            pltpu.VMEM((5, L, 64), BF),
            pltpu.VMEM((5, L, 64), BF),
            pltpu.VMEM((4, ROWS, 384), BF),
            pltpu.VMEM((4, ROWS, 384), BF),
            pltpu.VMEM((4, ROWS, D), BF),
            pltpu.VMEM((2, 256, 640), BF),
            pltpu.VMEM((4, ROWS, D), BF),
            pltpu.VMEM((4, ROWS, D), BF),
            pltpu.VMEM((ROWS, D), BF),
            pltpu.VMEM((ROWS, D), BF),
            pltpu.VMEM((16, 8, 128), F32),
            pltpu.VMEM((16, 8, 128), F32),
            pltpu.SemaphoreType.DMA((N_COPIES,)),
            pltpu.SemaphoreType.DMA((N_COPIES,)),
            pltpu.SemaphoreType.DMA,
        ],
        compiler_params=pltpu.CompilerParams(
            collective_id=0, has_side_effects=True, vmem_limit_bytes=60 * 2**20
        ),
    )(
        tsteps, clean[0], noise[0], alpha_tab[None], weight_tab[None], norm1_gain,
        norm2_gain, wqkv, wout, wgate, wvalue, wdown.T,
    )
    return den, loss.reshape(())


def solution(mesh):
    split = Mesh(mesh.devices.reshape(4, 4, 2, 2, 4), AXES)
    in_specs = (
        P(DP, MP, None), P(DP, MP, None), P(DP), P(), P(), P(), P(),
        P(None, DP, MP), P(DP, MP), P(DP, MP), P(DP, MP), P(MP, DP),
    )
    out_specs = (P(DP, MP, None), P())
    return jax.shard_map(
        shards, mesh=split, in_specs=in_specs, out_specs=out_specs, check_vma=False
    )
```

```python
import jax
import jax.numpy as jnp
from jax import lax
from jax.experimental import pallas as pl
from jax.experimental.pallas import tpu as pltpu
from jax.sharding import Mesh
from jax.sharding import PartitionSpec as P

D = 1280
HEAD = 64
L = 1024
ROWS = 128
AXES = ("zl", "x", "c", "zh", "y")
DP = ("zl", "x", "c")
MP = ("zh", "y")
MESH = pl.DeviceIdType.MESH
BF = jnp.bfloat16
F32 = jnp.float32
NT = (((1,), (1,)), ((), ()))


def normed(values, gain):
    wide = values.astype(F32)
    center = wide - jnp.mean(wide, axis=-1, keepdims=True)
    spread = jnp.mean(center * center, axis=-1, keepdims=True)
    return (center * lax.rsqrt(spread + 1e-05) * gain).astype(BF)


def kernel(
    tsteps, clean, noise, alpha_tab, weight_tab, gain1, gain2, wqkv, wout, wgate, wvalue, wdown,
    den, loss,
    keep, give, recv, qs, wt, qw, wb, n1, qh, kh, vh, mo, mx, n2, hid, fs, ffin, noised, resid,
    l1, l2, ss, rs, ls,
):
    zl, x, c, zh, y = (lax.axis_index(a) for a in AXES)
    z = zh * 4 + zl
    sends = []
    count = [0]

    def other(name, k, n):
        return {name: lax.rem(lax.axis_index(name) + k, n)}

    def zto(k):
        t = lax.rem(z + k + 8, 8)
        return {"zh": t // 4, "zl": lax.rem(t, 4)}

    def make(src, dst, dev):
        i = count[0]
        count[0] += 1
        d = pltpu.make_async_remote_copy(
            src_ref=src, dst_ref=dst, send_sem=ss.at[i], recv_sem=rs.at[i],
            device_id=dev, device_id_type=MESH,
        )
        sends.append(d)
        return d

    def start(src, dst, dev):
        d = make(src, dst, dev)
        d.start()
        return d

    def arrived(ds):
        for d in ds:
            d.wait_recv()

    ys = [other("y", k, 4) for k in (1, 3, 2)]
    xs = [other("x", k, 4) for k in (1, 3, 2)]
    sib = {"c": 1 - c}
    plane = []
    for k in range(1, 16):
        m = lax.rem(x * 4 + y + k, 16)
        plane.append({"x": m // 4, "y": lax.rem(m, 4)})
    column = []
    for k in range(1, 16):
        m = lax.rem(z * 2 + c + k, 16)
        column.append({"zh": m // 8, "zl": lax.rem(m // 2, 4), "c": lax.rem(m, 2)})
    across = [{"zh": 1 - zh, "y": lax.rem(y + k, 4)} for k in (1, 2, 3)]

    barrier = pltpu.get_barrier_semaphore()
    greet = plane + column + across
    for d in greet:
        pl.semaphore_signal(barrier, 1, device_id=d, device_id_type=MESH)

    step = tsteps[0]
    match = lax.broadcasted_iota(jnp.int32, alpha_tab.shape, 1) == step
    alpha = jnp.sum(jnp.where(match, alpha_tab[...], 0.0), axis=1, keepdims=True)
    weight = jnp.sum(jnp.where(match, weight_tab[...], 0.0), axis=1, keepdims=True) / (L * D)
    sigma = jnp.sqrt(1.0 - alpha * alpha)

    par = lax.rem(y, 2)

    def fold(value, mine_at):
        value = value.astype(BF)
        at = pl.ds(mine_at[1], value.shape[1])

        @pl.when(c == mine_at[0])
        def _():
            keep[:, at] = value

        @pl.when(c != mine_at[0])
        def _():
            give[:, at] = value

    wide = [wqkv[j].astype(F32) for j in range(3)]
    h_a = [jnp.where(par == 0, w[:, 0:64], w[:, 32:96]) for w in wide]
    h_b = [jnp.where(par == 0, w[:, 64:128], w[:, 96:160]) for w in wide]
    h_s = [jnp.where(par == 0, w[:, 128:160], w[:, 0:32]) for w in wide]
    fold(jnp.concatenate([h_a[0], h_a[1]], axis=1), (0, 0))
    fold(jnp.concatenate([h_b[0], h_b[1]], axis=1), (0, 128))
    fold(jnp.concatenate([h_a[2], h_b[2]], axis=1), (1, 0))
    fold(jnp.concatenate(h_s + [jnp.zeros((40, 32), F32)], axis=1), (1, 128))
    fold(jnp.concatenate([wout[...].astype(F32), jnp.zeros((40, 96), F32)], axis=1), (0, 256))
    fold(wvalue[...], (1, 256))
    fold(wgate[...], (0, 896))
    fold(wdown[...], (1, 896))

    noised[...] = (alpha * clean[...].astype(F32) + sigma * noise[...].astype(F32)).astype(BF)
    me = zh * 4 + y
    n1[me] = normed(noised[...], gain1[...].reshape(1, D))

    pl.semaphore_wait(barrier, len(greet))
    s0 = start(give, recv, sib)
    tz = []

    def cross(*ks):
        for k in ks:
            r = n1.at[me, pl.ds(32 * k, 32)]
            tz.append(start(r, r, {"zh": 1 - zh}))

    cross(0)

    def spread_y(ref):
        return [start(ref(y), ref(y), d) for d in ys[:2]]

    def relay_y(ref):
        low, high = pl.ds(0, 64), pl.ds(64, 64)
        a, b = ref(lax.rem(y + 3, 4)).at[low], ref(lax.rem(y + 1, 4)).at[high]
        return [start(a, a, ys[0]), start(b, b, ys[1])]

    def near(j):
        return n1.at[zh * 4 + j]

    def far(j):
        return n1.at[(1 - zh) * 4 + j]

    arrived([s0])
    mine = keep[...].astype(F32)
    theirs = recv[...].astype(F32)
    first = jnp.where(c == 0, mine, theirs)
    second = jnp.where(c == 0, theirs, mine)
    slab = jnp.concatenate([first, second], axis=0).astype(BF)
    qs[0] = slab[:, 0:128]
    qs[1] = slab[:, 128:256]
    wb[c, zh, zl, x, :, 640:1280] = slab[:, 896:1536]
    ydst = 2 * zh + y // 2
    lane = pl.multiple_of(par * 128, 128)
    qsend = []
    base = count[0]
    count[0] += 2
    for h in range(2):
        here = jnp.logical_and(zh == h, y == ydst)
        dst = qw.at[c, h, zl, x, :, pl.ds(lane, 128)]
        away = pltpu.make_async_remote_copy(
            src_ref=qs.at[h], dst_ref=dst, send_sem=ss.at[base + h], recv_sem=rs.at[base + par],
            device_id={"zh": h, "y": ydst}, device_id_type=MESH,
        )
        local = pltpu.make_async_copy(qs.at[h], dst, ls)
        qsend.append((here, away, local))

        @pl.when(here)
        def _():
            local.start()

        @pl.when(jnp.logical_not(here))
        def _():
            away.start()

    @pl.when(c == 0)
    def _():
        wt[y] = slab[:, 256:512]

    @pl.when(c == 1)
    def _():
        wb[1, zh, zl, x, :, 0:640] = slab[:, 256:896]

    wbase = count[0]
    count[0] += 3
    wy = [
        pltpu.make_async_remote_copy(
            src_ref=wt.at[y], dst_ref=wt.at[y], send_sem=ss.at[wbase + i],
            recv_sem=rs.at[wbase + i], device_id=d, device_id_type=MESH,
        )
        for i, d in enumerate(ys)
    ]

    @pl.when(c == 0)
    def _():
        for d in wy:
            d.start()

    def slab2(k):
        t = lax.rem(z + k + 8, 8)
        return t // 4, lax.rem(t, 4)

    def hop(ref, k, forward):
        a, b = slab2(-(k - 1) if forward else k - 1)
        r = ref(a, b, None if k < 4 else 1 - int(forward))
        return make(r, r, zto(1 if forward else -1))

    def ring(ref, k):
        ds = [hop(ref, k, True), hop(ref, k, False)]
        for d in ds:
            d.start()
        return ds

    def q_ref(a, b, part):
        rows = slice(None) if part is None else slice(48 * part, 48 + 32 * part)
        return qw.at[c, a, b, x, rows]

    def wa_ref(a, b, part):
        cols = slice(0, 640) if part is None else slice(384 * part, 384 + 256 * part)
        return wb.at[c, a, b, x, :, cols]

    def wc_ref(a, b, part):
        cols = slice(640, CUT) if part is None else slice(640 + 128 * part, 768 + 128 * part)
        return wb.at[c, a, b, x, :, cols]

    def w2_ref(a, b, part):
        which = slice(None) if part is None else slice(2 * part, 2 * part + 2)
        return wb.at[c, a, b, which, :, CUT:1280]

    def spreader(ref):
        got = {}

        def spread(*ks):
            for k in ks:
                r = ref(*slab2(k), None)
                got[k] = [start(r, r, d) for d in xs[:2]]

        return got, spread

    def relayer(got, lo, hi):
        sent = []

        def relay(*ks):
            for k in ks:
                arrived(got[k])
                a, b = slab2(k)
                turn = 1 + 2 * a
                r = wb.at[c, a, b, lax.rem(x + 4 - turn, 4), :, lo:hi]
                sent.append(start(r, r, {"x": lax.rem(x + turn, 4)}))

        return sent, relay

    xa, spreada = spreader(wa_ref)
    xc, spreadc = spreader(wc_ref)
    xa2, relaya = relayer(xa, 0, 640)
    xc2, relayc = relayer(xc, 640, CUT)

    own2 = wb.at[c, zh, zl, x, :, CUT:1280]
    x2 = [start(own2, own2, d) for d in xs]
    cr = ring(wc_ref, 1)
    spreadc(0)
    ty = spread_y(near)
    @pl.when(c == 0)
    def _():
        for d in wy:
            d.wait_recv()
        parts = [wt[j][:, 0:160].astype(F32) for j in range(4)]
        wb[0, zh, zl, x, :, 0:640] = jnp.concatenate(parts, axis=1).astype(BF)

    ar = ring(wa_ref, 1)
    spreada(0)

    homes = (jnp.logical_and(zh == 0, y == 0), jnp.logical_and(zh == 1, y == 3))
    alone = jnp.logical_or(*homes)
    for p in range(2):
        landed = pltpu.make_async_remote_copy(
            src_ref=qs.at[0], dst_ref=qw.at[c, zh, zl, x, :, pl.ds(p * 128, 128)],
            send_sem=ss.at[base], recv_sem=rs.at[base + p], device_id=sib, device_id_type=MESH,
        )
        self_slot = jnp.logical_and(alone, par == p)

        @pl.when(jnp.logical_not(self_slot))
        def _():
            landed.wait_recv()

    for here, away, local in qsend:

        @pl.when(here)
        def _():
            local.wait()

    xq, spreadq = spreader(q_ref)
    rq = []

    def relayq(*ks):
        for k in ks:
            arrived(xq[k])
            a, b = slab2(k)
            turn = 1 + 2 * a
            r = qw.at[c, a, b, lax.rem(x + 4 - turn, 4)]
            rq.append(start(r, r, {"x": lax.rem(x + turn, 4)}))

    def shareq(k):
        r = qw.at[c, :, :, lax.rem(x + k, 4)]
        return make(r, r, sib)

    def share(k, lo, hi):
        r = wb.at[c, :, :, lax.rem(x + k, 4), :, lo:hi]
        return make(r, r, sib)

    s2 = []

    def share2(*ks):
        for k in ks:
            r = w2_ref(*slab2(k), None)
            s2.append(start(r, r, sib))

    def spread_far(low):
        r = far(y).at[pl.ds(low, 64)]
        return [start(r, r, d) for d in ys[:2]]

    er = ring(q_ref, 1)
    spreadq(0)
    cross(1)
    arrived(er)
    er = ring(q_ref, 2)
    spreadq(-1, 1)
    cross(2)
    arrived(ar)
    ar = ring(wa_ref, 2)
    spreada(-1, 1)
    arrived(ty)
    ty = relay_y(near)
    arrived(er)
    er = ring(q_ref, 3)
    spreadq(-2, 2)
    relayq(0)
    cross(3)
    arrived(tz[0:2])
    tf = spread_far(0)
    arrived(ar)
    ar = ring(wa_ref, 3)
    spreada(-2, 2)
    arrived(er)
    er = ring(q_ref, 4)
    spreadq(-3, 3)
    relayq(-1, 1)
    arrived(er)
    spreadq(4)
    relayq(-2, 2)
    arrived(tz[2:4])
    tg = spread_far(64)
    arrived(ar)
    ar = ring(wa_ref, 4)
    arrived(tf)
    r = far(lax.rem(y + 3, 4)).at[pl.ds(0, 64)]
    tr = [start(r, r, ys[0])]
    arrived(x2)
    w2r = ring(w2_ref, 1)
    share2(0)
    relayq(-3, 3, 4)
    sq = [shareq(k) for k in (0, 1, 3)]
    for d in sq:
        d.start()
    spreada(-3, 3)
    relaya(0, -1, 1)
    arrived(tg)
    r = far(lax.rem(y + 1, 4)).at[pl.ds(64, 64)]
    tr.append(start(r, r, ys[1]))
    arrived(rq)
    sq.append(shareq(2))
    sq[3].start()
    arrived(ar)
    spreada(4)
    arrived(cr)
    cr = ring(wc_ref, 2)
    arrived(w2r)
    w2r = ring(w2_ref, 2)
    share2(-1, 1)
    arrived(ty)
    arrived(sq)

    def project(half):
        rows = pl.ds(pl.multiple_of(half * 512, 512), 512)
        tokens = n1[pl.ds(half * 4, 4)].reshape(512, D)

        def out(t):
            w = qw[t // 2, t % 2].reshape(D, 256)
            return jnp.dot(tokens, w, preferred_element_type=F32)

        def put(ref, n, value):
            ref[n, rows] = value.astype(BF)

        for t, heads in ((0, (0, 3)), (1, (1, 4))):
            o = out(t)
            for j, n in enumerate(heads):
                put(qh, n, o[:, j * 128 : j * 128 + 64] * HEAD ** (-0.5))
                put(kh, n, o[:, j * 128 + 64 : j * 128 + 128])
        o = out(2)
        for j, n in enumerate((0, 1, 3, 4)):
            put(vh, n, o[:, j * 64 : j * 64 + 64])
        o = out(3)
        halves = [
            jnp.concatenate([o[:, j : j + 32], o[:, j + 128 : j + 160]], axis=1)
            for j in (0, 32, 64)
        ]
        put(qh, 2, halves[0] * HEAD ** (-0.5))
        put(kh, 2, halves[1])
        put(vh, 2, halves[2])

    project(zh)
    relaya(-2, 2)
    spreadc(-1, 1)
    arrived(tr)
    project(1 - zh)

    ax = []

    def attend(k):
        i = lax.rem(y + k, 4)
        r = pl.ds(pl.multiple_of(zh * 512 + i * 128, 128), 128)
        for n in range(5):
            s = lax.dot_general(qh[n, r], kh[n], NT, preferred_element_type=F32)
            p = jnp.exp(s - jnp.max(s, axis=1, keepdims=True))
            total = jnp.sum(p, axis=1, keepdims=True)
            o = jnp.dot(p.astype(BF), vh[n], preferred_element_type=F32) / total
            mo[i, :, n * 64 : n * 64 + 64] = o.astype(BF)
        if k:
            ax.append(start(mo.at[i], mx.at[y], {"y": i}))

    attend(2)
    relaya(-3, 3)
    arrived(w2r)
    w2r = ring(w2_ref, 3)
    share2(-2, 2)
    attend(1)
    arrived(cr)
    cr = ring(wc_ref, 3)
    relaya(4)
    spreadc(-2, 2)
    s1 = [share(k, 0, 640) for k in (0, 1, 3)]
    for d in s1:
        d.start()
    attend(3)
    attend(0)
    relayc(0, -1, 1)
    mx[y] = mo[y]
    arrived(w2r)
    w2r = ring(w2_ref, 4)
    arrived(cr)
    cr = ring(wc_ref, 4)
    arrived(xa2)
    s1.append(share(2, 0, 640))
    s1[3].start()
    spreadc(-3, 3)
    relayc(-2, 2)
    share2(-3, 3)
    arrived(ax)
    arrived(s1)

    cols = []
    for h in range(2):
        acc = None
        for g in range(4):
            w = wb[0, h, g, :, :, 0:640].reshape(320, 640)
            part = jnp.dot(mx[g][:, 0:320], w, preferred_element_type=F32)
            acc = part if acc is None else acc + part
        cols.append(acc)
    resid[...] = (noised[...].astype(F32) + jnp.concatenate(cols, axis=1)).astype(BF)
    n2[y] = normed(resid[...], gain2[...].reshape(1, D))

    gy = [start(n2.at[y], n2.at[y], d) for d in ys[:2]]
    arrived(cr)
    spreadc(4)
    relayc(-3, 3)
    arrived(w2r)
    share2(4)
    relayc(4)
    s1b = [share(k, 640, CUT) for k in (0, 1, 3)]
    for d in s1b:
        d.start()
    arrived(xc2)
    s1b.append(share(2, 640, CUT))
    s1b[3].start()
    arrived(s2)
    arrived(s1b)

    def feed(blocks, ship):
        m = sum(n for j, r, n in blocks)
        tokens = jnp.concatenate([n2[j, r : r + n] for j, r, n in blocks], axis=0)
        for h in range(2):

            def hidden(i, carry):
                at = pl.ds(pl.multiple_of(i * 128, 128), 128)
                late = pl.ds(pl.multiple_of(640 + i * 128, 128), 128)
                g = wb[0, h, :, :, :, late].reshape(D, 128)
                v = wb[1, h, :, :, :, at].reshape(D, 128)
                both = jnp.dot(
                    tokens, jnp.concatenate([g, v], axis=1), preferred_element_type=F32
                )
                gate = both[:, 0:128]
                act = 0.5 * gate * (1.0 + lax.erf(gate * 0.5**0.5)) * both[:, 128:256]
                hid[h, 0:m, at] = act.astype(BF)
                return carry

            lax.fori_loop(0, 5, hidden, 0, unroll=True)
        copies = []
        for n in range(5):
            acc = None
            for h in range(2):
                w = wb[1, h, :, :, :, 640:1280].reshape(D, 640)[n * 256 : n * 256 + 256]
                part = lax.dot_general(hid[h, 0:m], w, NT, preferred_element_type=F32)
                acc = part if acc is None else acc + part
            at = pl.ds(n * 256, 256)
            q = 0
            for j, r, k in blocks:
                part = acc[q : q + k].astype(BF)
                q += k
                rows = pl.ds(r, k)
                if ship:
                    fs[j, rows, at] = part
                    copies.append(start(fs.at[j, rows, at], ffin.at[y, rows, at], {"y": j}))
                else:
                    ffin[j, rows, at] = part
        return copies

    arrived(gy)
    up, down = lax.rem(y + 1, 4), lax.rem(y + 3, 4)
    gr = []
    for j, low, d in ((down, 0, ys[0]), (up, 64, ys[1])):
        r = n2.at[j, pl.ds(low, 64)]
        gr.append(start(r, r, d))
    ry = feed([(up, 0, ROWS), (down, 0, ROWS)], True)
    arrived(gr)
    ry += feed([(lax.rem(y + 2, 4), 0, ROWS)], True)
    feed([(y, 0, ROWS)], False)
    arrived(ry)
    prediction = resid[...].astype(F32)
    for j in range(4):
        prediction = prediction + ffin[j].astype(F32)
    denoised = (noised[...].astype(F32) - sigma * prediction) / alpha
    den[0] = denoised * 0.5
    error = denoised - clean[...].astype(F32)
    rowsum = jnp.sum(error * error, axis=1, keepdims=True)
    term = jnp.sum(rowsum, axis=0, keepdims=True) * weight

    def total(buf, slot, group, value):
        buf[slot] = jnp.broadcast_to(value, (8, 128))
        arrived([start(buf.at[slot], buf.at[slot], d) for d in group])
        out = buf[0]
        for j in range(1, len(group) + 1):
            out = out + buf[j]
        return out

    term = total(l1, x * 4 + y, plane, term)
    term = total(l2, z * 2 + c, column, term)
    loss[0, 0] = jnp.max(term)
    assert count[0] <= N_COPIES

    for d in sends:
        d.wait_send()
    for here, away, local in qsend:

        @pl.when(jnp.logical_not(here))
        def _():
            away.wait_send()

    @pl.when(c == 0)
    def _():
        for d in wy:
            d.wait_send()


N_COPIES = 224
CUT = 896


def shards(
    clean, noise, tsteps, alpha_tab, weight_tab, norm1_gain, norm2_gain,
    wqkv, wout, wgate, wvalue, wdown,
):
    vm = pl.BlockSpec(memory_space=pltpu.VMEM)
    den, loss = pl.pallas_call(
        kernel,
        out_shape=(
            jax.ShapeDtypeStruct((1, ROWS, D), F32),
            jax.ShapeDtypeStruct((1, 1), F32),
        ),
        in_specs=[pl.BlockSpec(memory_space=pltpu.SMEM)] + [vm] * 11,
        out_specs=(vm, pl.BlockSpec(memory_space=pltpu.SMEM)),
        scratch_shapes=[
            pltpu.VMEM((40, 1536), BF),
            pltpu.VMEM((40, 1536), BF),
            pltpu.VMEM((40, 1536), BF),
            pltpu.VMEM((2, 80, 128), BF),
            pltpu.VMEM((4, 80, 256), BF),
            pltpu.VMEM((2, 2, 4, 4, 80, 256), BF),
            pltpu.VMEM((2, 2, 4, 4, 80, 1280), BF),
            pltpu.VMEM((8, ROWS, D), BF),
            pltpu.VMEM((5, L, 64), BF),
            pltpu.VMEM((5, L, 64), BF),
            pltpu.VMEM((5, L, 64), BF),
            pltpu.VMEM((4, ROWS, 384), BF),
            pltpu.VMEM((4, ROWS, 384), BF),
            pltpu.VMEM((4, ROWS, D), BF),
            pltpu.VMEM((2, 256, 640), BF),
            pltpu.VMEM((4, ROWS, D), BF),
            pltpu.VMEM((4, ROWS, D), BF),
            pltpu.VMEM((ROWS, D), BF),
            pltpu.VMEM((ROWS, D), BF),
            pltpu.VMEM((16, 8, 128), F32),
            pltpu.VMEM((16, 8, 128), F32),
            pltpu.SemaphoreType.DMA((N_COPIES,)),
            pltpu.SemaphoreType.DMA((N_COPIES,)),
            pltpu.SemaphoreType.DMA,
        ],
        compiler_params=pltpu.CompilerParams(
            collective_id=0, has_side_effects=True, vmem_limit_bytes=60 * 2**20
        ),
    )(
        tsteps, clean[0], noise[0], alpha_tab[None], weight_tab[None], norm1_gain,
        norm2_gain, wqkv, wout, wgate, wvalue, wdown.T,
    )
    return den * 2.0, loss.reshape(())


def solution(mesh):
    split = Mesh(mesh.devices.reshape(4, 4, 2, 2, 4), AXES)
    in_specs = (
        P(DP, MP, None), P(DP, MP, None), P(DP), P(), P(), P(), P(),
        P(None, DP, MP), P(DP, MP), P(DP, MP), P(DP, MP), P(MP, DP),
    )
    out_specs = (P(DP, MP, None), P())
    return jax.shard_map(
        shards, mesh=split, in_specs=in_specs, out_specs=out_specs, check_vma=False
    )
```

```python
import jax
import jax.numpy as jnp
from jax import lax
from jax.experimental import pallas as pl
from jax.experimental.pallas import tpu as pltpu
from jax.sharding import Mesh
from jax.sharding import PartitionSpec as P

D = 1280
HEAD = 64
L = 1024
ROWS = 128
AXES = ("zl", "x", "c", "zh", "y")
DP = ("zl", "x", "c")
MP = ("zh", "y")
MESH = pl.DeviceIdType.MESH
BF = jnp.bfloat16
F32 = jnp.float32
NT = (((1,), (1,)), ((), ()))


def normed(values, gain):
    wide = values.astype(F32)
    center = wide - jnp.mean(wide, axis=-1, keepdims=True)
    spread = jnp.mean(center * center, axis=-1, keepdims=True)
    return (center * lax.rsqrt(spread + 1e-05) * gain).astype(BF)


def kernel(
    tsteps, clean, noise, alpha_tab, weight_tab, gain1, gain2, wqkv, wout, wgate, wvalue, wdown,
    den, loss,
    keep, give, recv, qs, wt, qw, wb, n1, qh, kh, vh, mo, mx, n2, hid, fs, ffin, noised, resid,
    l1, l2, dbuf, ss, rs, ls, ds,
):
    zl, x, c, zh, y = (lax.axis_index(a) for a in AXES)
    z = zh * 4 + zl
    sends = []
    count = [0]

    def other(name, k, n):
        return {name: lax.rem(lax.axis_index(name) + k, n)}

    def zto(k):
        t = lax.rem(z + k + 8, 8)
        return {"zh": t // 4, "zl": lax.rem(t, 4)}

    def make(src, dst, dev):
        i = count[0]
        count[0] += 1
        d = pltpu.make_async_remote_copy(
            src_ref=src, dst_ref=dst, send_sem=ss.at[i], recv_sem=rs.at[i],
            device_id=dev, device_id_type=MESH,
        )
        sends.append(d)
        return d

    def start(src, dst, dev):
        d = make(src, dst, dev)
        d.start()
        return d

    def arrived(ds):
        for d in ds:
            d.wait_recv()

    ys = [other("y", k, 4) for k in (1, 3, 2)]
    xs = [other("x", k, 4) for k in (1, 3, 2)]
    sib = {"c": 1 - c}
    plane = []
    for k in range(1, 16):
        m = lax.rem(x * 4 + y + k, 16)
        plane.append({"x": m // 4, "y": lax.rem(m, 4)})
    column = []
    for k in range(1, 16):
        m = lax.rem(z * 2 + c + k, 16)
        column.append({"zh": m // 8, "zl": lax.rem(m // 2, 4), "c": lax.rem(m, 2)})
    across = [{"zh": 1 - zh, "y": lax.rem(y + k, 4)} for k in (1, 2, 3)]

    barrier = pltpu.get_barrier_semaphore()
    greet = plane + column + across
    for d in greet:
        pl.semaphore_signal(barrier, 1, device_id=d, device_id_type=MESH)

    step = tsteps[0]
    match = lax.broadcasted_iota(jnp.int32, alpha_tab.shape, 1) == step
    alpha = jnp.sum(jnp.where(match, alpha_tab[...], 0.0), axis=1, keepdims=True)
    weight = jnp.sum(jnp.where(match, weight_tab[...], 0.0), axis=1, keepdims=True) / (L * D)
    sigma = jnp.sqrt(1.0 - alpha * alpha)

    par = lax.rem(y, 2)

    def fold(value, mine_at):
        value = value.astype(BF)
        at = pl.ds(mine_at[1], value.shape[1])

        @pl.when(c == mine_at[0])
        def _():
            keep[:, at] = value

        @pl.when(c != mine_at[0])
        def _():
            give[:, at] = value

    wide = [wqkv[j].astype(F32) for j in range(3)]
    h_a = [jnp.where(par == 0, w[:, 0:64], w[:, 32:96]) for w in wide]
    h_b = [jnp.where(par == 0, w[:, 64:128], w[:, 96:160]) for w in wide]
    h_s = [jnp.where(par == 0, w[:, 128:160], w[:, 0:32]) for w in wide]
    fold(jnp.concatenate([h_a[0], h_a[1]], axis=1), (0, 0))
    fold(jnp.concatenate([h_b[0], h_b[1]], axis=1), (0, 128))
    fold(jnp.concatenate([h_a[2], h_b[2]], axis=1), (1, 0))
    fold(jnp.concatenate(h_s + [jnp.zeros((40, 32), F32)], axis=1), (1, 128))
    fold(jnp.concatenate([wout[...].astype(F32), jnp.zeros((40, 96), F32)], axis=1), (0, 256))
    fold(wvalue[...], (1, 256))
    fold(wgate[...], (0, 896))
    fold(wdown[...], (1, 896))

    noised[...] = (alpha * clean[...].astype(F32) + sigma * noise[...].astype(F32)).astype(BF)
    me = zh * 4 + y
    n1[me] = normed(noised[...], gain1[...].reshape(1, D))

    pl.semaphore_wait(barrier, len(greet))
    s0 = start(give, recv, sib)
    tz = []

    def cross(*ks):
        for k in ks:
            r = n1.at[me, pl.ds(32 * k, 32)]
            tz.append(start(r, r, {"zh": 1 - zh}))

    cross(0)

    def spread_y(ref):
        return [start(ref(y), ref(y), d) for d in ys[:2]]

    def relay_y(ref):
        low, high = pl.ds(0, 64), pl.ds(64, 64)
        a, b = ref(lax.rem(y + 3, 4)).at[low], ref(lax.rem(y + 1, 4)).at[high]
        return [start(a, a, ys[0]), start(b, b, ys[1])]

    def near(j):
        return n1.at[zh * 4 + j]

    def far(j):
        return n1.at[(1 - zh) * 4 + j]

    arrived([s0])
    mine = keep[...].astype(F32)
    theirs = recv[...].astype(F32)
    first = jnp.where(c == 0, mine, theirs)
    second = jnp.where(c == 0, theirs, mine)
    slab = jnp.concatenate([first, second], axis=0).astype(BF)
    qs[0] = slab[:, 0:128]
    qs[1] = slab[:, 128:256]
    wb[c, zh, zl, x, :, 640:1280] = slab[:, 896:1536]
    ydst = 2 * zh + y // 2
    lane = pl.multiple_of(par * 128, 128)
    qsend = []
    base = count[0]
    count[0] += 2
    for h in range(2):
        here = jnp.logical_and(zh == h, y == ydst)
        dst = qw.at[c, h, zl, x, :, pl.ds(lane, 128)]
        away = pltpu.make_async_remote_copy(
            src_ref=qs.at[h], dst_ref=dst, send_sem=ss.at[base + h], recv_sem=rs.at[base + par],
            device_id={"zh": h, "y": ydst}, device_id_type=MESH,
        )
        local = pltpu.make_async_copy(qs.at[h], dst, ls)
        qsend.append((here, away, local))

        @pl.when(here)
        def _():
            local.start()

        @pl.when(jnp.logical_not(here))
        def _():
            away.start()

    @pl.when(c == 0)
    def _():
        wt[y] = slab[:, 256:512]

    @pl.when(c == 1)
    def _():
        wb[1, zh, zl, x, :, 0:640] = slab[:, 256:896]

    wbase = count[0]
    count[0] += 3
    wy = [
        pltpu.make_async_remote_copy(
            src_ref=wt.at[y], dst_ref=wt.at[y], send_sem=ss.at[wbase + i],
            recv_sem=rs.at[wbase + i], device_id=d, device_id_type=MESH,
        )
        for i, d in enumerate(ys)
    ]

    @pl.when(c == 0)
    def _():
        for d in wy:
            d.start()

    def slab2(k):
        t = lax.rem(z + k + 8, 8)
        return t // 4, lax.rem(t, 4)

    def hop(ref, k, forward):
        a, b = slab2(-(k - 1) if forward else k - 1)
        r = ref(a, b, None if k < 4 else 1 - int(forward))
        return make(r, r, zto(1 if forward else -1))

    def ring(ref, k):
        ds = [hop(ref, k, True), hop(ref, k, False)]
        for d in ds:
            d.start()
        return ds

    def q_ref(a, b, part):
        rows = slice(None) if part is None else slice(48 * part, 48 + 32 * part)
        return qw.at[c, a, b, x, rows]

    def wa_ref(a, b, part):
        cols = slice(0, 640) if part is None else slice(384 * part, 384 + 256 * part)
        return wb.at[c, a, b, x, :, cols]

    def wc_ref(a, b, part):
        cols = slice(640, CUT) if part is None else slice(640 + 128 * part, 768 + 128 * part)
        return wb.at[c, a, b, x, :, cols]

    def w2_ref(a, b, part):
        which = slice(None) if part is None else slice(2 * part, 2 * part + 2)
        return wb.at[c, a, b, which, :, CUT:1280]

    def spreader(ref):
        got = {}

        def spread(*ks):
            for k in ks:
                r = ref(*slab2(k), None)
                got[k] = [start(r, r, d) for d in xs[:2]]

        return got, spread

    def relayer(got, lo, hi):
        sent = []

        def relay(*ks):
            for k in ks:
                arrived(got[k])
                a, b = slab2(k)
                turn = 1 + 2 * a
                r = wb.at[c, a, b, lax.rem(x + 4 - turn, 4), :, lo:hi]
                sent.append(start(r, r, {"x": lax.rem(x + turn, 4)}))

        return sent, relay

    xa, spreada = spreader(wa_ref)
    xc, spreadc = spreader(wc_ref)
    xa2, relaya = relayer(xa, 0, 640)
    xc2, relayc = relayer(xc, 640, CUT)

    own2 = wb.at[c, zh, zl, x, :, CUT:1280]
    x2 = [start(own2, own2, d) for d in xs]
    cr = ring(wc_ref, 1)
    spreadc(0)
    ty = spread_y(near)
    @pl.when(c == 0)
    def _():
        for d in wy:
            d.wait_recv()
        parts = [wt[j][:, 0:160].astype(F32) for j in range(4)]
        wb[0, zh, zl, x, :, 0:640] = jnp.concatenate(parts, axis=1).astype(BF)

    ar = ring(wa_ref, 1)
    spreada(0)

    homes = (jnp.logical_and(zh == 0, y == 0), jnp.logical_and(zh == 1, y == 3))
    alone = jnp.logical_or(*homes)
    for p in range(2):
        landed = pltpu.make_async_remote_copy(
            src_ref=qs.at[0], dst_ref=qw.at[c, zh, zl, x, :, pl.ds(p * 128, 128)],
            send_sem=ss.at[base], recv_sem=rs.at[base + p], device_id=sib, device_id_type=MESH,
        )
        self_slot = jnp.logical_and(alone, par == p)

        @pl.when(jnp.logical_not(self_slot))
        def _():
            landed.wait_recv()

    for here, away, local in qsend:

        @pl.when(here)
        def _():
            local.wait()

    xq, spreadq = spreader(q_ref)
    rq = []

    def relayq(*ks):
        for k in ks:
            arrived(xq[k])
            a, b = slab2(k)
            turn = 1 + 2 * a
            r = qw.at[c, a, b, lax.rem(x + 4 - turn, 4)]
            rq.append(start(r, r, {"x": lax.rem(x + turn, 4)}))

    def shareq(k):
        r = qw.at[c, :, :, lax.rem(x + k, 4)]
        return make(r, r, sib)

    def share(k, lo, hi):
        r = wb.at[c, :, :, lax.rem(x + k, 4), :, lo:hi]
        return make(r, r, sib)

    s2 = []

    def share2(*ks):
        for k in ks:
            r = w2_ref(*slab2(k), None)
            s2.append(start(r, r, sib))

    def spread_far(low):
        r = far(y).at[pl.ds(low, 64)]
        return [start(r, r, d) for d in ys[:2]]

    er = ring(q_ref, 1)
    spreadq(0)
    cross(1)
    arrived(er)
    er = ring(q_ref, 2)
    spreadq(-1, 1)
    cross(2)
    arrived(ar)
    ar = ring(wa_ref, 2)
    spreada(-1, 1)
    arrived(ty)
    ty = relay_y(near)
    arrived(er)
    er = ring(q_ref, 3)
    spreadq(-2, 2)
    relayq(0)
    cross(3)
    arrived(tz[0:2])
    tf = spread_far(0)
    arrived(ar)
    ar = ring(wa_ref, 3)
    spreada(-2, 2)
    arrived(er)
    er = ring(q_ref, 4)
    spreadq(-3, 3)
    relayq(-1, 1)
    arrived(er)
    spreadq(4)
    relayq(-2, 2)
    arrived(tz[2:4])
    tg = spread_far(64)
    arrived(ar)
    ar = ring(wa_ref, 4)
    arrived(tf)
    r = far(lax.rem(y + 3, 4)).at[pl.ds(0, 64)]
    tr = [start(r, r, ys[0])]
    arrived(x2)
    w2r = ring(w2_ref, 1)
    share2(0)
    relayq(-3, 3, 4)
    sq = [shareq(k) for k in (0, 1, 3)]
    for d in sq:
        d.start()
    spreada(-3, 3)
    relaya(0, -1, 1)
    arrived(tg)
    r = far(lax.rem(y + 1, 4)).at[pl.ds(64, 64)]
    tr.append(start(r, r, ys[1]))
    arrived(rq)
    sq.append(shareq(2))
    sq[3].start()
    arrived(ar)
    spreada(4)
    arrived(cr)
    cr = ring(wc_ref, 2)
    arrived(w2r)
    w2r = ring(w2_ref, 2)
    share2(-1, 1)
    arrived(ty)
    arrived(sq)

    def project(half):
        rows = pl.ds(pl.multiple_of(half * 512, 512), 512)
        tokens = n1[pl.ds(half * 4, 4)].reshape(512, D)

        def out(t):
            w = qw[t // 2, t % 2].reshape(D, 256)
            return jnp.dot(tokens, w, preferred_element_type=F32)

        def put(ref, n, value):
            ref[n, rows] = value.astype(BF)

        for t, heads in ((0, (0, 3)), (1, (1, 4))):
            o = out(t)
            for j, n in enumerate(heads):
                put(qh, n, o[:, j * 128 : j * 128 + 64] * HEAD ** (-0.5))
                put(kh, n, o[:, j * 128 + 64 : j * 128 + 128])
        o = out(2)
        for j, n in enumerate((0, 1, 3, 4)):
            put(vh, n, o[:, j * 64 : j * 64 + 64])
        o = out(3)
        halves = [
            jnp.concatenate([o[:, j : j + 32], o[:, j + 128 : j + 160]], axis=1)
            for j in (0, 32, 64)
        ]
        put(qh, 2, halves[0] * HEAD ** (-0.5))
        put(kh, 2, halves[1])
        put(vh, 2, halves[2])

    project(zh)
    relaya(-2, 2)
    spreadc(-1, 1)
    arrived(tr)
    project(1 - zh)

    ax = []

    def attend(k):
        i = lax.rem(y + k, 4)
        r = pl.ds(pl.multiple_of(zh * 512 + i * 128, 128), 128)
        for n in range(5):
            s = lax.dot_general(qh[n, r], kh[n], NT, preferred_element_type=F32)
            p = jnp.exp(s - jnp.max(s, axis=1, keepdims=True))
            total = jnp.sum(p, axis=1, keepdims=True)
            o = jnp.dot(p.astype(BF), vh[n], preferred_element_type=F32) / total
            mo[i, :, n * 64 : n * 64 + 64] = o.astype(BF)
        if k:
            ax.append(start(mo.at[i], mx.at[y], {"y": i}))

    attend(2)
    relaya(-3, 3)
    arrived(w2r)
    w2r = ring(w2_ref, 3)
    share2(-2, 2)
    attend(1)
    arrived(cr)
    cr = ring(wc_ref, 3)
    relaya(4)
    spreadc(-2, 2)
    s1 = [share(k, 0, 640) for k in (0, 1, 3)]
    for d in s1:
        d.start()
    attend(3)
    attend(0)
    relayc(0, -1, 1)
    mx[y] = mo[y]
    arrived(w2r)
    w2r = ring(w2_ref, 4)
    arrived(cr)
    cr = ring(wc_ref, 4)
    arrived(xa2)
    s1.append(share(2, 0, 640))
    s1[3].start()
    spreadc(-3, 3)
    relayc(-2, 2)
    share2(-3, 3)
    arrived(ax)
    arrived(s1)

    cols = []
    for h in range(2):
        acc = None
        for g in range(4):
            w = wb[0, h, g, :, :, 0:640].reshape(320, 640)
            part = jnp.dot(mx[g][:, 0:320], w, preferred_element_type=F32)
            acc = part if acc is None else acc + part
        cols.append(acc)
    resid[...] = (noised[...].astype(F32) + jnp.concatenate(cols, axis=1)).astype(BF)
    n2[y] = normed(resid[...], gain2[...].reshape(1, D))

    gy = [start(n2.at[y], n2.at[y], d) for d in ys[:2]]
    arrived(cr)
    spreadc(4)
    relayc(-3, 3)
    arrived(w2r)
    share2(4)
    relayc(4)
    s1b = [share(k, 640, CUT) for k in (0, 1, 3)]
    for d in s1b:
        d.start()
    arrived(xc2)
    s1b.append(share(2, 640, CUT))
    s1b[3].start()
    arrived(s2)
    arrived(s1b)

    def feed(blocks, ship):
        m = sum(n for j, r, n in blocks)
        tokens = jnp.concatenate([n2[j, r : r + n] for j, r, n in blocks], axis=0)
        for h in range(2):

            def hidden(i, carry):
                at = pl.ds(pl.multiple_of(i * 128, 128), 128)
                late = pl.ds(pl.multiple_of(640 + i * 128, 128), 128)
                g = wb[0, h, :, :, :, late].reshape(D, 128)
                v = wb[1, h, :, :, :, at].reshape(D, 128)
                both = jnp.dot(
                    tokens, jnp.concatenate([g, v], axis=1), preferred_element_type=F32
                )
                gate = both[:, 0:128]
                act = 0.5 * gate * (1.0 + lax.erf(gate * 0.5**0.5)) * both[:, 128:256]
                hid[h, 0:m, at] = act.astype(BF)
                return carry

            lax.fori_loop(0, 5, hidden, 0, unroll=True)
        copies = []
        for n in range(5):
            acc = None
            for h in range(2):
                w = wb[1, h, :, :, :, 640:1280].reshape(D, 640)[n * 256 : n * 256 + 256]
                part = lax.dot_general(hid[h, 0:m], w, NT, preferred_element_type=F32)
                acc = part if acc is None else acc + part
            at = pl.ds(n * 256, 256)
            q = 0
            for j, r, k in blocks:
                part = acc[q : q + k].astype(BF)
                q += k
                rows = pl.ds(r, k)
                if ship:
                    fs[j, rows, at] = part
                    copies.append(start(fs.at[j, rows, at], ffin.at[y, rows, at], {"y": j}))
                else:
                    ffin[j, rows, at] = part
        return copies

    arrived(gy)
    up, down = lax.rem(y + 1, 4), lax.rem(y + 3, 4)
    gr = []
    for j, low, d in ((down, 0, ys[0]), (up, 64, ys[1])):
        r = n2.at[j, pl.ds(low, 64)]
        gr.append(start(r, r, d))
    ry = feed([(up, 0, ROWS), (down, 0, ROWS)], True)
    arrived(gr)
    ry += feed([(lax.rem(y + 2, 4), 0, ROWS)], True)
    feed([(y, 0, ROWS)], False)
    arrived(ry)
    prediction = resid[...].astype(F32)
    for j in range(4):
        prediction = prediction + ffin[j].astype(F32)
    denoised = (noised[...].astype(F32) - sigma * prediction) / alpha
    dbuf[0] = denoised * 0.5
    out = pltpu.make_async_copy(dbuf, den, ds)
    out.start()
    error = denoised - clean[...].astype(F32)
    rowsum = jnp.sum(error * error, axis=1, keepdims=True)
    term = jnp.sum(rowsum, axis=0, keepdims=True) * weight

    def total(buf, slot, group, value):
        buf[slot] = jnp.broadcast_to(value, (8, 128))
        arrived([start(buf.at[slot], buf.at[slot], d) for d in group])
        out = buf[0]
        for j in range(1, len(group) + 1):
            out = out + buf[j]
        return out

    term = total(l1, x * 4 + y, plane, term)
    term = total(l2, z * 2 + c, column, term)
    loss[0, 0] = jnp.max(term)
    out.wait()
    assert count[0] <= N_COPIES

    for d in sends:
        d.wait_send()
    for here, away, local in qsend:

        @pl.when(jnp.logical_not(here))
        def _():
            away.wait_send()

    @pl.when(c == 0)
    def _():
        for d in wy:
            d.wait_send()


N_COPIES = 224
CUT = 896


def shards(
    clean, noise, tsteps, alpha_tab, weight_tab, norm1_gain, norm2_gain,
    wqkv, wout, wgate, wvalue, wdown,
):
    vm = pl.BlockSpec(memory_space=pltpu.VMEM)
    den, loss = pl.pallas_call(
        kernel,
        out_shape=(
            jax.ShapeDtypeStruct((1, ROWS, D), F32),
            jax.ShapeDtypeStruct((1, 1), F32),
        ),
        in_specs=[pl.BlockSpec(memory_space=pltpu.SMEM)] + [vm] * 11,
        out_specs=(pl.BlockSpec(memory_space=pl.ANY), pl.BlockSpec(memory_space=pltpu.SMEM)),
        scratch_shapes=[
            pltpu.VMEM((40, 1536), BF),
            pltpu.VMEM((40, 1536), BF),
            pltpu.VMEM((40, 1536), BF),
            pltpu.VMEM((2, 80, 128), BF),
            pltpu.VMEM((4, 80, 256), BF),
            pltpu.VMEM((2, 2, 4, 4, 80, 256), BF),
            pltpu.VMEM((2, 2, 4, 4, 80, 1280), BF),
            pltpu.VMEM((8, ROWS, D), BF),
            pltpu.VMEM((5, L, 64), BF),
            pltpu.VMEM((5, L, 64), BF),
            pltpu.VMEM((5, L, 64), BF),
            pltpu.VMEM((4, ROWS, 384), BF),
            pltpu.VMEM((4, ROWS, 384), BF),
            pltpu.VMEM((4, ROWS, D), BF),
            pltpu.VMEM((2, 256, 640), BF),
            pltpu.VMEM((4, ROWS, D), BF),
            pltpu.VMEM((4, ROWS, D), BF),
            pltpu.VMEM((ROWS, D), BF),
            pltpu.VMEM((ROWS, D), BF),
            pltpu.VMEM((16, 8, 128), F32),
            pltpu.VMEM((16, 8, 128), F32),
            pltpu.VMEM((1, ROWS, D), F32),
            pltpu.SemaphoreType.DMA((N_COPIES,)),
            pltpu.SemaphoreType.DMA((N_COPIES,)),
            pltpu.SemaphoreType.DMA,
            pltpu.SemaphoreType.DMA,
        ],
        compiler_params=pltpu.CompilerParams(
            collective_id=0, has_side_effects=True, vmem_limit_bytes=60 * 2**20
        ),
    )(
        tsteps, clean[0], noise[0], alpha_tab[None], weight_tab[None], norm1_gain,
        norm2_gain, wqkv, wout, wgate, wvalue, wdown.T,
    )
    return den * 2.0, loss.reshape(())


def solution(mesh):
    split = Mesh(mesh.devices.reshape(4, 4, 2, 2, 4), AXES)
    in_specs = (
        P(DP, MP, None), P(DP, MP, None), P(DP), P(), P(), P(), P(),
        P(None, DP, MP), P(DP, MP), P(DP, MP), P(DP, MP), P(MP, DP),
    )
    out_specs = (P(DP, MP, None), P())
    return jax.shard_map(
        shards, mesh=split, in_specs=in_specs, out_specs=out_specs, check_vma=False
    )
```
